512 devices in a mesh: din: 16 (over z), dout: 32 (over y, x, core).
Axes of the slice: x: 4, y: 4, z: 16, core: 2. Of those that a mesh axis runs over, the one named last changes fastest.
Arguments:
- inputs: bfloat16 [2048, 8192], P('dout', 'din'), may hold values from -6 to 6
- cotangent: bfloat16 [2048, 28672], P('din', 'dout'), may hold values from -6 to 6
- codes: int32 [2, 1024, 28672], P(None, 'din', 'dout'), may hold values from 0 to 255
- codebooks: float32 [2, 256, 8], replicated, may hold values from -6 to 6
- scales: float32 [28672], P('dout'), may hold values from 0.5 to 2
- book_mean: float32 [2, 256, 8], replicated, may hold values from -3 to 3
- book_var: float32 [2, 256, 8], replicated, may hold values from 0.1 to 1
- scale_mean: float32 [28672], P('dout'), may hold values from -3 to 3
- scale_var: float32 [28672], P('dout'), may hold values from 0.1 to 1
Outputs:
- grad_input: bfloat16 [2048, 8192], P('dout', 'din')
- book_grad: float32 [2, 256, 8], replicated
- new_books: float32 [2, 256, 8], replicated
- new_book_mean: float32 [2, 256, 8], replicated
- new_book_var: float32 [2, 256, 8], replicated
- new_scales: float32 [28672], P('dout')
- new_scale_mean: float32 [28672], P('dout')
- new_scale_var: float32 [28672], P('dout')
The draws below stay inside these ranges and needn't reach their ends.
Inputs may be any that keep to these rules, and one draw needn't show every extreme that they name: codes[b, g, o] names the entry of codebook b used for input features 8 * g to 8 * g + 7 of output o.
All inputs are finite; a program needn't handle non-finite values.
Results may differ from the reference program's by a relative error of at most 0.0057.
Values may be sent and summed in bfloat16 or wider, within the bound.
A program may use at most 64 MiB of HBM per device.

```python
import math
import jax
import jax.numpy as jnp
from jax import lax

DIN = 8192
DOUT = 28672
KCODE = 256
BOOKS = 2
GROUP = 8
TOKENS = 2048
N_DOUT = 32


def touch_ends(drawn, own_key, least, largest):
    longest = drawn.shape.index(max(drawn.shape))
    spots = []
    for shift in (0, 1):
        where = [jax.random.randint(jax.random.fold_in(own_key, axis), (), 0, length) for axis, length in enumerate(drawn.shape)]
        where[longest] = (where[longest] + shift) % drawn.shape[longest]
        spots.append(tuple(where))
    return drawn.at[spots[0]].set(least).at[spots[1]].set(largest)


def shard_levels(rng, shape, pieces, low, top_value):
    level, own = 1.0, jax.random.fold_in(rng, 6)
    for dim, shards_of in pieces:
        draws = jnp.exp(jax.random.uniform(jax.random.fold_in(own, dim), (shards_of,), jnp.float32, low / len(pieces), top_value / len(pieces)))
        level = level * jnp.repeat(draws, shape[dim] // shards_of).reshape([-1 if axis == dim else 1 for axis in range(len(shape))])
    return level


def noise(stream_key, extent, deviation, limit, shards=(), kind=jnp.bfloat16):
    entries = jax.random.normal(stream_key, extent, jnp.float32) * deviation
    if len(shards) > 0:
        entries = shard_levels(stream_key, extent, shards, -0.22, 0.18) * entries
    return jnp.clip(entries, min=-limit, max=limit).astype(kind)


def setup_inputs(seed: int = 0) -> dict:
    key_of = jax.random.split(jax.random.key(seed), 10)
    inputs = noise(key_of[0], (TOKENS, DIN), 1.0, 6.0, ((0, 32), (1, 16)))
    cotangent = noise(key_of[1], (TOKENS, DOUT), 1.0, 6.0, ((0, 16), (1, 32)))
    codes = touch_ends(jax.random.randint(key_of[2], (BOOKS, DIN // GROUP, DOUT), 0, KCODE), jax.random.fold_in(key_of[2], 1), 0, KCODE - 1).astype(jnp.int32)
    codebooks = noise(key_of[3], (BOOKS, KCODE, GROUP), 1.0, 6.0, (), jnp.float32)
    scales = jnp.clip(jnp.exp(math.log(2.0) - 1.3862944 * jax.random.uniform(key_of[4], (DOUT,), jnp.float32) ** shard_levels(key_of[4], (DOUT,), ((0, 32),), -0.2, 0.2)), 0.5, 2.0)
    book_mean = noise(key_of[5], (BOOKS, KCODE, GROUP), 0.5, 3.0, (), jnp.float32)
    book_var = jnp.clip(jnp.exp(jax.random.uniform(key_of[6], (BOOKS, KCODE, GROUP), jnp.float32, math.log(0.1), math.log(1.0))), 0.1, 1.0)
    scale_mean = noise(key_of[7], (DOUT,), 0.5, 3.0, ((0, 32),), jnp.float32)
    scale_var = jnp.clip(jnp.exp(math.log(1.0) - 2.3025851 * jax.random.uniform(key_of[8], (DOUT,), jnp.float32) ** shard_levels(key_of[8], (DOUT,), ((0, 32),), -0.2, 0.2)), 0.1, 1.0)
    return {"inputs": inputs, "cotangent": cotangent, "codes": codes, "codebooks": codebooks, "scales": scales, "book_mean": book_mean, "book_var": book_var, "scale_mean": scale_mean, "scale_var": scale_var}


beta_one = 0.9
beta_two = 0.999
adam_rate = 0.01
adam_eps = 1e-08
corr_one = 1.0 - 0.9 ** 10
corr_two = 1.0 - 0.999 ** 10

def adam_step(param, mean_old, var_old, gradient):
    mean_new = beta_one * mean_old + (1.0 - beta_one) * gradient
    var_new = beta_two * var_old + (1.0 - beta_two) * gradient * gradient
    update = mean_new / corr_one / (jnp.sqrt(var_new / corr_two) + adam_eps)
    return (param - adam_rate * update, mean_new, var_new)

def reference(inputs, cotangent, codes, codebooks, scales, book_mean, book_var, scale_mean, scale_var):
    norm_factor = 1.0 / (2.0 * DOUT) ** 0.5
    loss_scale = (TOKENS * DIN / 4096.0) ** 0.5
    coef = scales * norm_factor
    rounded = lax.optimization_barrier(codebooks.astype(jnp.bfloat16)).astype(jnp.float32)
    width = DOUT // N_DOUT
    groups = DIN // GROUP

    def block_step(state_tuple, block_index):
        gx_total, grad_total = state_tuple
        first_col = block_index * width
        code_block = lax.dynamic_slice_in_dim(codes, first_col, width, 2)
        coef_block = lax.dynamic_slice_in_dim(coef, first_col, width, 0)
        gy_block = lax.dynamic_slice_in_dim(cotangent, first_col, width, 1)
        decoded = rounded[0][code_block[0]] + rounded[1][code_block[1]]
        decoded = decoded.transpose(0, 2, 1).reshape(DIN, width)
        weights = (decoded * coef_block).astype(jnp.bfloat16)
        grad_w = jnp.dot(inputs.T, gy_block, preferred_element_type=jnp.float32)
        gx_total = gx_total + jnp.dot(gy_block, weights.T, preferred_element_type=jnp.float32)
        scaled = lax.optimization_barrier((grad_w * coef_block).astype(jnp.bfloat16)).astype(jnp.float32)
        flattened = scaled.reshape(groups, GROUP, width).transpose(0, 2, 1).reshape(-1, GROUP)
        book_terms = [jax.ops.segment_sum(flattened, code_block[which_book].reshape(-1), num_segments=KCODE) for which_book in range(BOOKS)]
        grad_total = grad_total + jnp.stack(book_terms)
        scale_part = lax.optimization_barrier(jnp.sum(decoded * grad_w, axis=0))
        return ((gx_total, grad_total), scale_part)
    start_state = (jnp.zeros((TOKENS, DIN), jnp.float32), jnp.zeros((BOOKS, KCODE, GROUP), jnp.float32))
    (gx_total, grad_total), scale_parts = lax.scan(block_step, start_state, jnp.arange(N_DOUT, dtype=jnp.int32))
    grad_input = gx_total.astype(jnp.bfloat16)
    book_grad = grad_total / loss_scale
    scale_grad = scale_parts.reshape(DOUT) * norm_factor / loss_scale
    new_books, new_book_mean, new_book_var = adam_step(codebooks, book_mean, book_var, book_grad)
    new_scales, new_scale_mean, new_scale_var = adam_step(scales, scale_mean, scale_var, scale_grad)
    return (grad_input, book_grad, new_books, new_book_mean, new_book_var, new_scales, new_scale_mean, new_scale_var)
```

```python
import functools

import jax
import jax.numpy as jnp
from jax import lax
from jax.experimental import pallas as pl
from jax.experimental.pallas import tpu as pltpu
from jax.sharding import PartitionSpec as P

DIN = 8192
DOUT = 28672
KCODE = 256
BOOKS = 2
GROUP = 8
TOKENS = 2048

beta_one = 0.9
beta_two = 0.999
adam_rate = 0.01
adam_eps = 1e-08
corr_one = 1.0 - 0.9**10
corr_two = 1.0 - 0.999**10

LANES = 128
LOW = 8
HIGH = KCODE // LOW


def adam_step(param, mean_old, var_old, gradient):
    mean_new = beta_one * mean_old + (1.0 - beta_one) * gradient
    var_new = beta_two * var_old + (1.0 - beta_two) * gradient * gradient
    update = mean_new / corr_one / (jnp.sqrt(var_new / corr_two) + adam_eps)
    return (param - adam_rate * update, mean_new, var_new)


def kernel(
    nz, nd, x_hbm, gy_hbm, codes, table, coef, gx_out, book_out, scale_out,
    gyf, xf, xt, wts, dec, gw, gkeep, gst, gpr, rss, rsr, hloc, hpair, hsum, hplane, hz, hfin, sown, sz,
    loc_sem, gy_send, gy_recv, x_send, x_recv, p_send, p_recv, r_send, r_recv,
    hp_send, hp_recv, hx_send, hx_recv, hz_send, hz_recv, hf_send, hf_recv, s_send, s_recv,
):
    chips = nd // 2
    half = nz // 2
    nc = gyf.shape[0]
    cl = (nc + 1) // 2
    rows = gy_hbm.shape[0]
    xrows = x_hbm.shape[0]
    feats = x_hbm.shape[1]
    groups = codes.shape[1]
    iz = lax.axis_index("din")
    jd = lax.axis_index("dout")
    chip = jd // 2
    core = jd % 2
    mate = jd + 1 - 2 * core
    right = lax.rem(iz + 1, nz)
    left = lax.rem(iz + nz - 1, nz)
    f32 = jnp.float32
    bf16 = jnp.bfloat16

    def remote(src, dst, ssem, rsem, din=None, dout=None):
        where = {}
        if din is not None:
            where["din"] = din
        if dout is not None:
            where["dout"] = dout
        return pltpu.make_async_remote_copy(
            src_ref=src, dst_ref=dst, send_sem=ssem, recv_sem=rsem,
            device_id=where, device_id_type=pl.DeviceIdType.MESH,
        )

    def rows_of(block):
        return pl.ds(pl.multiple_of(block * rows, rows), rows)

    for c in range(nc):
        pltpu.make_async_copy(
            gy_hbm.at[:, pl.ds(c * LANES, LANES)], gyf.at[c, rows_of(iz)], loc_sem.at[c]
        ).start()
    pltpu.make_async_copy(x_hbm, xf.at[jd], loc_sem.at[nc]).start()

    barrier = pltpu.get_barrier_semaphore()
    for k in range(1, nz):
        pl.semaphore_signal(barrier, 1, device_id={"din": lax.rem(iz + k, nz)}, device_id_type=pl.DeviceIdType.MESH)
    for k in range(1, chips):
        pl.semaphore_signal(
            barrier, 1, device_id={"dout": 2 * lax.rem(chip + k, chips) + core}, device_id_type=pl.DeviceIdType.MESH
        )
    pl.semaphore_signal(barrier, 1, device_id={"dout": mate}, device_id_type=pl.DeviceIdType.MESH)
    chip_by = chip + 1 - 2 * (chip % 2)
    pl.semaphore_signal(barrier, 1, device_id={"dout": 2 * chip_by + 1 - core}, device_id_type=pl.DeviceIdType.MESH)

    for c in range(nc):
        pltpu.make_async_copy(
            gy_hbm.at[:, pl.ds(c * LANES, LANES)], gyf.at[c, rows_of(iz)], loc_sem.at[c]
        ).wait()
    pltpu.make_async_copy(x_hbm, xf.at[jd], loc_sem.at[nc]).wait()
    pl.semaphore_wait(barrier, nz - 1 + chips - 1 + 2)

    def send_right(s, c):
        block = lax.rem(iz - s + nz, nz)
        part = gyf.at[c, rows_of(block)]
        return remote(part, part, gy_send.at[0, s], gy_recv.at[0, s, c], din=right)

    def send_left(s, c):
        block = lax.rem(iz + s, nz)
        part = gyf.at[c, rows_of(block)]
        return remote(part, part, gy_send.at[1, s], gy_recv.at[1, s, c], din=left)

    for c in range(nc):
        if half > 1 or c < cl:
            send_right(0, c).start()
        if half > 1 or c >= cl:
            send_left(0, c).start()

    def x_copy(k, dev, sem):
        return remote(xf.at[k], xf.at[k], x_send.at[sem], x_recv.at[k], dout=dev)

    x_copy(jd, mate, 2 * chips - 2).start()
    for k in range(1, chips):
        x_copy(jd, 2 * lax.rem(chip + k, chips) + core, k - 1).start()

    def x_forward(k):
        src = 2 * lax.rem(chip + chips - k, chips) + core
        x_copy(src, mate, chips - 1 + k - 1).wait_recv()
        x_copy(src, mate, chips - 1 + k - 1).start()

    def ring(r, c, last=False):
        bl = lax.rem(iz - r + nz, nz)
        br = lax.rem(iz + r, nz)
        if not last or c < cl:
            part = gyf.at[c, rows_of(bl)]
            remote(part, part, gy_send.at[0, 0], gy_recv.at[0, r - 1, c], din=right).wait_recv()
            if not last:
                if c < cl:
                    send_right(r, c).start()
                else:
                    @pl.when(r < half - 1)
                    def _():
                        send_right(r, c).start()
        if not last or c >= cl:
            part = gyf.at[c, rows_of(br)]
            remote(part, part, gy_send.at[1, 0], gy_recv.at[1, r - 1, c], din=left).wait_recv()
            if not last:
                if c >= cl:
                    send_left(r, c).start()
                else:
                    @pl.when(r < half - 1)
                    def _():
                        send_left(r, c).start()

    def lookup(which, idx):
        low = lax.bitwise_and(idx, LANES - 1)
        first = jnp.take_along_axis(table[which, :, 0:LANES], low, axis=1, mode="promise_in_bounds")
        second = jnp.take_along_axis(table[which, :, LANES:KCODE], low, axis=1, mode="promise_in_bounds")
        return jnp.where(idx >= LANES, second, first)

    def decode(c):
        cols = pl.ds(c * LANES, LANES)
        co = coef[0:1, cols]

        @pl.loop(0, groups // 8)
        def _(q):
            at = pl.ds(pl.multiple_of(q * 8, 8), 8)
            c0 = codes[0, at, cols]
            c1 = codes[1, at, cols]
            out = []
            for g in range(8):
                d = lookup(0, jnp.broadcast_to(c0[g : g + 1], (8, LANES))) + lookup(
                    1, jnp.broadcast_to(c1[g : g + 1], (8, LANES))
                )
                out.append(d)
            d = jnp.concatenate(out, axis=0)
            where = pl.ds(pl.multiple_of(q * 64, 64), 64)
            dec[where, cols] = d
            wts[where, cols] = (d * co).astype(bf16)

    def g_part(block, slot):
        lhs = jnp.concatenate([gyf[c, rows_of(block)] for c in range(nc)], axis=1)
        g = lax.dot_general(lhs, wts[...], (((1,), (1,)), ((), ())), preferred_element_type=f32)
        g = g.reshape(2, rows // 2, feats)
        gkeep[slot] = g
        gst[slot] = g.astype(bf16)
        remote(gst.at[slot, 1 - core], gpr.at[slot], p_send.at[slot], p_recv.at[slot], dout=mate).start()

    def g_pass(block, slot):
        remote(gst.at[slot, 1 - core], gpr.at[slot], p_send.at[slot], p_recv.at[slot], dout=mate).wait_recv()
        total = gkeep[slot, core] + gpr[slot].astype(f32)
        rss[slot] = total.astype(bf16)

        @pl.when(block == chip)
        def _():
            pltpu.make_async_copy(rss.at[slot], rsr.at[chip], r_send.at[slot]).start()

        @pl.when(block != chip)
        def _():
            remote(rss.at[slot], rsr.at[chip], r_send.at[slot], r_recv.at[chip], dout=2 * block + core).start()

    def left_of(r):
        return lax.rem(iz - r + nz, nz)

    def right_of(r):
        return lax.rem(iz + r, nz)

    def gw_pair(q, first=False):
        b0, b1 = right_of(q), left_of(q + 1)
        lhs = jnp.concatenate([xt[b0], xt[b1]], axis=1)
        for c in range(nc):
            gw_chunk(lhs, b0, b1, c, first)

    def gw_chunk(lhs, b0, b1, c, first=False):
        rhs = jnp.concatenate([gyf[c, rows_of(b0)], gyf[c, rows_of(b1)]], axis=0)
        d = jnp.dot(lhs, rhs, preferred_element_type=f32)
        cols = pl.ds(c * LANES, LANES)
        if first:
            gw[:, cols] = d
        else:
            gw[:, cols] += d

    def transpose_x(k):
        blk = xf[pl.ds(2 * k, 2)].reshape(rows, feats)
        xt[k] = jnp.transpose(blk)

    if half > 1:
        for c in range(nc):
            ring(1, c)
            decode(c)
    else:
        for c in range(nc):
            decode(c)
    g_part(iz, 0)

    fw = list(range(1, chips))
    if half > 2:
        for c in range(nc):
            ring(2, c)
            for k in fw[c::nc]:
                x_forward(k)
            if c == nc // 2 - 1:
                g_part(left_of(1), 1)
            if c == nc - 1:
                g_part(right_of(1), 2)
    else:
        for k in fw:
            x_forward(k)
        if half > 1:
            g_part(left_of(1), 1)
            g_part(right_of(1), 2)
    g_pass(iz, 0)

    def x_ready(k):
        src = 2 * k + 1 - core
        x_copy(src, mate, 0).wait_recv()
        transpose_x(k)

    if half > 3:
        for c in range(nc):
            ring(3, c)
            for k in range(c, chips, nc):
                x_ready(k)
            if c == 2 % nc:
                g_part(left_of(2), 3)
            if c == 4 % nc:
                g_part(right_of(2), 4)
        g_pass(left_of(1), 1)
        g_pass(right_of(1), 2)
    else:
        for k in range(chips):
            x_ready(k)
        for r in range(2, half):
            g_part(left_of(r), 2 * r - 1)
            g_part(right_of(r), 2 * r)
        for r in range(1, min(half, 2)):
            g_pass(left_of(r), 2 * r - 1)
            g_pass(right_of(r), 2 * r)

    gw_pair(0, True)
    if half > 4:
        @pl.loop(4, half)
        def _(r):
            for c in range(nc):
                ring(r, c)
                if c == 1:
                    g_part(left_of(r - 1), 2 * r - 3)
                if c == 2:
                    g_part(right_of(r - 1), 2 * r - 2)
                if c == 3:
                    gw_pair(r - 2)
                if c == 4:
                    @pl.when(r == 4)
                    def _():
                        gw_pair(1)
                if c == 5:
                    g_pass(left_of(r - 2), 2 * r - 5)
                    g_pass(right_of(r - 2), 2 * r - 4)

        done = half - 2
    else:
        done = 1

    if half > 3:
        g_part(left_of(half - 1), 2 * half - 3)
        g_part(right_of(half - 1), 2 * half - 2)
        g_pass(left_of(half - 2), 2 * half - 5)
        g_pass(right_of(half - 2), 2 * half - 4)
    for q in range(done, half - 1):
        gw_pair(q)
    if half > 2:
        g_pass(left_of(half - 1), 2 * half - 3)
        g_pass(right_of(half - 1), 2 * half - 2)

    hloc[...] = jnp.zeros_like(hloc)
    sown[...] = jnp.zeros_like(sown)
    order = []
    for k in range(cl):
        order.append(k)
        if cl + k < nc:
            order.append(cl + k)
    b0, b1 = right_of(half - 1), left_of(half)
    lhs = jnp.concatenate([xt[b0], xt[b1]], axis=1)
    row_low = lax.broadcasted_iota(jnp.int32, (LOW * 8, LANES), 0) // 8
    row_high = lax.broadcasted_iota(jnp.int32, (HIGH, LANES), 0)

    def finish(c):
        cols = pl.ds(c * LANES, LANES)
        sown[c : c + 1, :] = jnp.sum(dec[:, cols] * gw[:, cols], axis=0, keepdims=True)
        co = coef[0:1, cols]

        @pl.loop(0, groups // 8)
        def _(q):
            at = pl.ds(pl.multiple_of(q * 8, 8), 8)
            s = gw[pl.ds(pl.multiple_of(q * 64, 64), 64), cols] * co
            for b in range(BOOKS):
                cd = codes[b, at, cols]
                lo = lax.bitwise_and(cd, LOW - 1)
                hi = lax.shift_right_logical(cd, 3)
                a, o = [], []
                for g in range(8):
                    sg = s[8 * g : 8 * g + 8]
                    rep = jnp.concatenate([sg] * LOW, axis=0)
                    lo_b = jnp.broadcast_to(lo[g : g + 1], (LOW * 8, LANES))
                    a.append(jnp.where(lo_b == row_low, rep, 0.0).astype(bf16))
                    hi_b = jnp.broadcast_to(hi[g : g + 1], (HIGH, LANES))
                    o.append(jnp.where(hi_b == row_high, 1.0, 0.0).astype(bf16))
                left_m = jnp.concatenate(a, axis=1)
                right_m = jnp.concatenate(o, axis=1)
                hloc[b] += lax.dot_general(
                    left_m, right_m, (((1,), (1,)), ((), ())), preferred_element_type=f32
                )

    for c in order:
        ring(half, c, last=True)
        gw_chunk(lhs, b0, b1, c)
        if c == order[-1]:
            g_part(left_of(half), 2 * half - 1)
        finish(c)

    def s_copy(k):
        dev = lax.rem(iz + k, nz)
        return remote(sown, sz.at[iz], s_send.at[k - 1], s_recv.at[iz], din=dev)

    for k in range(1, nz):
        s_copy(k).start()

    pair = remote(hloc.at[1 - core], hpair, hp_send, hp_recv, dout=mate)
    pair.start()
    g_pass(left_of(half), 2 * half - 1)
    pair.wait_recv()
    both = hloc[core] + hpair[...]
    hsum[0] = both[0 : LOW * 4]
    hsum[1] = both[LOW * 4 : LOW * 8]

    def h_copy(k):
        other = lax.rem(chip + k, chips)
        return remote(
            hsum.at[other % 2], hplane.at[chip], hx_send.at[k - 1], hx_recv.at[chip], dout=2 * other + core
        )

    for k in range(1, chips):
        h_copy(k).start()
    hplane[chip] = hsum[chip % 2]
    for k in range(1, chips):
        src = lax.rem(chip + chips - k, chips)
        remote(hsum.at[0], hplane.at[src], hx_send.at[0], hx_recv.at[src], dout=2 * src + core).wait_recv()
    hz[iz] = jnp.sum(hplane[...], axis=0)

    def z_copy(k):
        dev = lax.rem(iz + k, nz)
        return remote(hz.at[iz], hz.at[iz], hz_send.at[k - 1], hz_recv.at[iz], din=dev)

    for k in range(1, nz):
        z_copy(k).start()

    sz[iz] = sown[...]
    for k in range(1, nz):
        src = lax.rem(iz + nz - k, nz)
        remote(sown, sz.at[src], s_send.at[0], s_recv.at[src], din=src).wait_recv()
    scale_out[...] = jnp.sum(sz[...], axis=0)

    for k in range(1, chips):
        src = lax.rem(chip + chips - k, chips)
        remote(rss.at[0], rsr.at[src], r_send.at[0], r_recv.at[src], dout=2 * src + core).wait_recv()
    slot_own = 0
    dist = lax.rem(chip - iz + nz, nz)
    slot_own = jnp.where(dist == 0, 0, jnp.where(dist < half, 2 * dist, 2 * (nz - dist) - 1))
    pltpu.make_async_copy(rss.at[slot_own], rsr.at[chip], r_send.at[slot_own]).wait()
    acc = rsr[0].astype(f32)
    for k in range(1, chips):
        acc = acc + rsr[k].astype(f32)
    gx_out[...] = acc

    for k in range(1, nz):
        src = lax.rem(iz + nz - k, nz)
        remote(hz.at[src], hz.at[src], hz_send.at[0], hz_recv.at[src], din=src).wait_recv()
    mine = 2 * core + chip % 2
    hfin[mine] = jnp.sum(hz[...], axis=0)

    def f_copy(k):
        if k == 0:
            dev = mate
        elif k == 1:
            dev = 2 * chip_by + core
        else:
            dev = 2 * chip_by + 1 - core
        return remote(hfin.at[mine], hfin.at[mine], hf_send.at[k], hf_recv.at[mine], dout=dev)

    for k in range(3):
        f_copy(k).start()
    for k in range(1, 4):
        src = lax.rem(mine + k, 4)
        remote(hfin.at[src], hfin.at[src], hf_send.at[0], hf_recv.at[src], dout=mate).wait_recv()
    book_out[...] = hfin[...]

    for s in range(half):
        wr = gyf.at[pl.ds(0, nc if s < half - 1 else cl), rows_of(left_of(s))]
        remote(wr, wr, gy_send.at[0, s], gy_recv.at[0, s, 0], din=right).wait_send()
        if s < half - 1:
            wl = gyf.at[:, rows_of(right_of(s))]
        else:
            wl = gyf.at[pl.ds(cl, nc - cl), rows_of(right_of(s))]
        if s < half - 1 or nc > cl:
            remote(wl, wl, gy_send.at[1, s], gy_recv.at[1, s, 0], din=left).wait_send()
    for k in range(2 * chips - 1):
        x_copy(jd, mate, k).wait_send()
    for k in range(1, nz):
        s_copy(k).wait_send()
        z_copy(k).wait_send()
    for k in range(1, chips):
        h_copy(k).wait_send()
    pair.wait_send()
    for k in range(3):
        f_copy(k).wait_send()
    for k in range(nz):
        remote(gst.at[k, 1 - core], gpr.at[k], p_send.at[k], p_recv.at[k], dout=mate).wait_send()

        @pl.when(k != slot_own)
        def _():
            remote(rss.at[k], rsr.at[chip], r_send.at[k], r_recv.at[chip], dout=mate).wait_send()


def fused(nz, nd, x, gy, codes, table, coef):
    xrows, feats = x.shape
    rows, outs = gy.shape
    nc = outs // LANES
    chips = nd // 2
    half = nz // 2
    bf16, f32 = jnp.bfloat16, jnp.float32
    V = pltpu.VMEM
    D = pltpu.SemaphoreType.DMA
    vm = pl.BlockSpec(memory_space=pltpu.VMEM)
    anyspec = pl.BlockSpec(memory_space=pl.ANY)
    tile = (LOW * 4, HIGH)
    scratch = [
        V((nc, rows * nz, LANES), bf16),
        V((nd, xrows, feats), bf16),
        V((nz, feats, rows), bf16),
        V((feats, outs), bf16),
        V((feats, outs), f32),
        V((feats, outs), f32),
        V((nz, 2, rows // 2, feats), f32),
        V((nz, 2, rows // 2, feats), bf16),
        V((nz, rows // 2, feats), bf16),
        V((nz, rows // 2, feats), bf16),
        V((chips, rows // 2, feats), bf16),
        V((BOOKS, LOW * 8, HIGH), f32),
        V((LOW * 8, HIGH), f32),
        V((2,) + tile, f32),
        V((chips,) + tile, f32),
        V((nz,) + tile, f32),
        V((4,) + tile, f32),
        V((8, LANES), f32),
        V((nz, 8, LANES), f32),
        D((nc + 1,)),
        D((2, half)),
        D((2, half, nc)),
        D((2 * chips - 1,)),
        D((nd,)),
        D((nz,)),
        D((nz,)),
        D((nz,)),
        D((chips,)),
        D(()),
        D(()),
        D((chips,)),
        D((chips,)),
        D((nz,)),
        D((nz,)),
        D((3,)),
        D((4,)),
        D((nz,)),
        D((nz,)),
    ]
    return pl.pallas_call(
        functools.partial(kernel, nz, nd),
        out_shape=(
            jax.ShapeDtypeStruct((xrows, feats), f32),
            jax.ShapeDtypeStruct((4,) + tile, f32),
            jax.ShapeDtypeStruct((8, LANES), f32),
        ),
        in_specs=[anyspec, anyspec, vm, vm, vm],
        out_specs=(vm, vm, vm),
        scratch_shapes=scratch,
        compiler_params=pltpu.CompilerParams(
            collective_id=0, has_side_effects=True, vmem_limit_bytes=60 * 1024 * 1024
        ),
        name="fused",
    )(x, gy, codes, table, coef)


def local(nz, nd, inputs, cotangent, codes, codebooks, scales, book_mean, book_var, scale_mean, scale_var):
    norm_factor = 1.0 / (2.0 * DOUT) ** 0.5
    loss_scale = (TOKENS * DIN / 4096.0) ** 0.5
    coef = scales * norm_factor
    outs = scales.shape[0]
    table = jnp.transpose(codebooks, (0, 2, 1)).astype(jnp.bfloat16).astype(jnp.float32)
    gx, book, scale = fused(nz, nd, inputs, cotangent, codes, table, coef.reshape(1, outs))
    book = book.reshape(BOOKS, LOW, GROUP, HIGH)
    grad_sums = jnp.transpose(book, (0, 3, 1, 2)).reshape(BOOKS, KCODE, GROUP)
    book_grad = grad_sums / loss_scale
    scale_grad = scale[: outs // LANES].reshape(outs) * norm_factor / loss_scale
    new_books, new_book_mean, new_book_var = adam_step(codebooks, book_mean, book_var, book_grad)
    new_scales, new_scale_mean, new_scale_var = adam_step(scales, scale_mean, scale_var, scale_grad)
    return (
        gx.astype(jnp.bfloat16),
        book_grad,
        new_books,
        new_book_mean,
        new_book_var,
        new_scales,
        new_scale_mean,
        new_scale_var,
    )


def solution(mesh):
    nz, nd = mesh.shape["din"], mesh.shape["dout"]
    in_specs = (
        P("dout", "din"),
        P("din", "dout"),
        P(None, "din", "dout"),
        P(),
        P("dout"),
        P(),
        P(),
        P("dout"),
        P("dout"),
    )
    out_specs = (P("dout", "din"), P(), P(), P(), P(), P("dout"), P("dout"), P("dout"))
    return jax.shard_map(
        functools.partial(local, nz, nd), mesh=mesh, in_specs=in_specs, out_specs=out_specs, check_vma=False
    )
```

```python
import functools

import jax
import jax.numpy as jnp
from jax import lax
from jax.experimental import pallas as pl
from jax.experimental.pallas import tpu as pltpu
from jax.sharding import PartitionSpec as P

DIN = 8192
DOUT = 28672
KCODE = 256
BOOKS = 2
GROUP = 8
TOKENS = 2048

beta_one = 0.9
beta_two = 0.999
adam_rate = 0.01
adam_eps = 1e-08
corr_one = 1.0 - 0.9**10
corr_two = 1.0 - 0.999**10

LANES = 128
LOW = 8
HBITS = 5
SKEW = 1
UNROLL = 16
HIGH = KCODE // LOW


def adam_step(param, mean_old, var_old, gradient):
    mean_new = beta_one * mean_old + (1.0 - beta_one) * gradient
    var_new = beta_two * var_old + (1.0 - beta_two) * gradient * gradient
    update = mean_new / corr_one / (jnp.sqrt(var_new / corr_two) + adam_eps)
    return (param - adam_rate * update, mean_new, var_new)


def kernel(
    nz, nd, x_hbm, gy_hbm, codes_hbm, books_hbm, scales_hbm, gx_out, book_out, scale_out,
    codes, books, scales, gyf, xf, xt, wts, dec, gw, table, gkeep, gst, gpr, rss, rsr, hloc, hbk, hplane, hz, hfin, sown, sz,
    loc_sem, gy_send, gy_recv, x_send, x_recv, p_send, p_recv, r_send, r_recv,
    hx_send, hx_recv, hz_send, hz_recv, hf_send, hf_recv, s_send, s_recv,
):
    chips = nd // 2
    half = nz // 2
    nc = gyf.shape[0]
    early = list(range((nc + 1) // 2))
    late = list(range((nc + 1) // 2, nc))
    goes_right = [k % 2 == 0 for k in range(nc)]
    n_right = sum(goes_right)
    skew = min(SKEW, half - 1)
    rows = gy_hbm.shape[0]
    xrows = x_hbm.shape[0]
    feats = x_hbm.shape[1]
    groups = codes.shape[1]
    iz = lax.axis_index("din")
    jd = lax.axis_index("dout")
    chip = jd // 2
    core = jd % 2
    mate = jd + 1 - 2 * core
    right = lax.rem(iz + 1, nz)
    left = lax.rem(iz + nz - 1, nz)
    f32 = jnp.float32
    bf16 = jnp.bfloat16

    def remote(src, dst, ssem, rsem, din=None, dout=None):
        where = {}
        if din is not None:
            where["din"] = din
        if dout is not None:
            where["dout"] = dout
        return pltpu.make_async_remote_copy(
            src_ref=src, dst_ref=dst, send_sem=ssem, recv_sem=rsem,
            device_id=where, device_id_type=pl.DeviceIdType.MESH,
        )

    def rows_of(block):
        return pl.ds(pl.multiple_of(block * rows, rows), rows)

    for c in range(nc):
        pltpu.make_async_copy(
            gy_hbm.at[:, pl.ds(c * LANES, LANES)], gyf.at[c, rows_of(iz)], loc_sem.at[c]
        ).start()
    pltpu.make_async_copy(x_hbm, xf.at[jd], loc_sem.at[nc]).start()
    operands = ((codes_hbm, codes), (books_hbm, books), (scales_hbm, scales))
    for n, (src, dst) in enumerate(operands):
        pltpu.make_async_copy(src, dst, loc_sem.at[nc + 1 + n]).start()

    barrier = pltpu.get_barrier_semaphore()
    for k in range(1, nz):
        pl.semaphore_signal(barrier, 1, device_id={"din": lax.rem(iz + k, nz)}, device_id_type=pl.DeviceIdType.MESH)
    for k in range(1, nd):
        pl.semaphore_signal(barrier, 1, device_id={"dout": lax.rem(jd + k, nd)}, device_id_type=pl.DeviceIdType.MESH)

    norm_factor = 1.0 / (2.0 * DOUT) ** 0.5
    def coef_of(c):
        return scales[pl.ds(c * LANES, LANES)].reshape(1, LANES) * norm_factor

    def lookup(which, idx):
        low = lax.bitwise_and(idx, LANES - 1)
        first = jnp.take_along_axis(table[which, :, 0:LANES], low, axis=1, mode="promise_in_bounds")
        second = jnp.take_along_axis(table[which, :, LANES:KCODE], low, axis=1, mode="promise_in_bounds")
        return jnp.where(idx >= LANES, second, first)

    unroll = min(UNROLL, groups)

    def decode(c):
        cols = pl.ds(c * LANES, LANES)
        co = coef_of(c)

        @pl.loop(0, groups // unroll)
        def _(q):
            at = pl.ds(pl.multiple_of(q * unroll, unroll), unroll)
            c0 = codes[0, at, cols]
            c1 = codes[1, at, cols]
            out = []
            for g in range(unroll):
                d = lookup(0, jnp.broadcast_to(c0[g : g + 1], (8, LANES))) + lookup(
                    1, jnp.broadcast_to(c1[g : g + 1], (8, LANES))
                )
                out.append(d)
            d = jnp.concatenate(out, axis=0)
            where = pl.ds(pl.multiple_of(q * unroll * 8, unroll * 8), unroll * 8)
            dec[where, cols] = d
            wts[where, cols] = (d * co).astype(bf16)

    for c in range(nc):
        pltpu.make_async_copy(
            gy_hbm.at[:, pl.ds(c * LANES, LANES)], gyf.at[c, rows_of(iz)], loc_sem.at[c]
        ).wait()
    pltpu.make_async_copy(x_hbm, xf.at[jd], loc_sem.at[nc]).wait()
    pl.semaphore_wait(barrier, nz - 1 + nd - 1)

    def send_right(s, c):
        block = lax.rem(iz - s + nz, nz)
        part = gyf.at[c, rows_of(block)]
        return remote(part, part, gy_send.at[0, s], gy_recv.at[0, s, c], din=right)

    def send_left(s, c):
        block = lax.rem(iz + s, nz)
        part = gyf.at[c, rows_of(block)]
        return remote(part, part, gy_send.at[1, s], gy_recv.at[1, s, c], din=left)

    def send_own(c):
        if half > 1 or goes_right[c]:
            send_right(0, c).start()
        if half > 1 or not goes_right[c]:
            send_left(0, c).start()

    for c in range(nc):
        send_own(c)

    def x_copy(k, dev, sem):
        return remote(xf.at[k], xf.at[k], x_send.at[sem], x_recv.at[k], dout=dev)

    x_copy(jd, mate, 2 * chips - 2).start()
    for k in range(1, chips):
        x_copy(jd, 2 * lax.rem(chip + k, chips) + core, k - 1).start()

    def x_forward(k):
        src = 2 * lax.rem(chip + chips - k, chips) + core
        x_copy(src, mate, chips - 1 + k - 1).wait_recv()
        x_copy(src, mate, chips - 1 + k - 1).start()

    def ring(r, c):
        bl = lax.rem(iz - r + nz, nz)
        br = lax.rem(iz + r, nz)
        if r < half or goes_right[c]:
            part = gyf.at[c, rows_of(bl)]
            remote(part, part, gy_send.at[0, 0], gy_recv.at[0, r - 1, c], din=right).wait_recv()
            if r < half - 1 or (r == half - 1 and goes_right[c]):
                send_right(r, c).start()
        if r < half or not goes_right[c]:
            part = gyf.at[c, rows_of(br)]
            remote(part, part, gy_send.at[1, 0], gy_recv.at[1, r - 1, c], din=left).wait_recv()
            if r < half - 1 or (r == half - 1 and not goes_right[c]):
                send_left(r, c).start()

    def g_dot(block, chunks):
        lhs = jnp.concatenate([gyf[c, rows_of(block)] for c in chunks], axis=1)
        rhs = wts[:, pl.ds(chunks[0] * LANES, len(chunks) * LANES)]
        return lax.dot_general(lhs, rhs, (((1,), (1,)), ((), ())), preferred_element_type=f32)

    def g_early(block, slot):
        gkeep[slot] = g_dot(block, early).reshape(2, rows // 2, feats)

    def g_late(block, slot):
        g = gkeep[slot] + g_dot(block, late).reshape(2, rows // 2, feats)
        gkeep[slot] = g
        gst[slot] = g.astype(bf16)
        remote(gst.at[slot, 1 - core], gpr.at[slot], p_send.at[slot], p_recv.at[slot], dout=mate).start()

    def g_pass(block, slot):
        remote(gst.at[slot, 1 - core], gpr.at[slot], p_send.at[slot], p_recv.at[slot], dout=mate).wait_recv()
        total = gkeep[slot, core] + gpr[slot].astype(f32)
        rss[slot] = total.astype(bf16)

        @pl.when(block == chip)
        def _():
            pltpu.make_async_copy(rss.at[slot], rsr.at[chip], r_send.at[slot]).start()

        @pl.when(block != chip)
        def _():
            remote(rss.at[slot], rsr.at[chip], r_send.at[slot], r_recv.at[chip], dout=2 * block + core).start()

    def left_of(r):
        return lax.rem(iz - r + nz, nz)

    def right_of(r):
        return lax.rem(iz + r, nz)

    def gw_pair(q, chunks):
        b0, b1 = right_of(q), left_of(q + 1)
        lhs = jnp.concatenate([xt[b0], xt[b1]], axis=1)
        for c in chunks:
            rhs = jnp.concatenate([gyf[c, rows_of(b0)], gyf[c, rows_of(b1)]], axis=0)
            d = jnp.dot(lhs, rhs, preferred_element_type=f32)
            cols = pl.ds(c * LANES, LANES)
            if q == 0:
                gw[:, cols] = d
            else:
                gw[:, cols] += d

    def transpose_x(k):
        blk = xf[pl.ds(2 * k, 2)].reshape(rows, feats)
        xt[k] = jnp.transpose(blk)

    def x_ready(k):
        src = 2 * k + 1 - core
        x_copy(src, mate, 0).wait_recv()
        transpose_x(k)

    hloc[...] = jnp.zeros_like(hloc)
    sown[...] = jnp.zeros_like(sown)
    rows16 = lax.broadcasted_iota(jnp.int32, (16, LANES), 0)
    row_low = [(rows16 // 8 + 2 * n).astype(f32).astype(bf16) for n in range(LOW // 2)]
    row_high = [(rows16 + 16 * n).astype(f32).astype(bf16) for n in range(HIGH // 16)]
    zero16 = jnp.zeros((16, LANES), bf16)
    one16 = jnp.ones((16, LANES), bf16)

    def finish(c):
        cols = pl.ds(c * LANES, LANES)
        sown[c : c + 1, :] = jnp.sum(dec[:, cols] * gw[:, cols], axis=0, keepdims=True)
        co = coef_of(c)

        @pl.loop(0, groups // unroll)
        def _(q):
            at = pl.ds(pl.multiple_of(q * unroll, unroll), unroll)
            s = gw[pl.ds(pl.multiple_of(q * unroll * 8, unroll * 8), unroll * 8), cols] * co
            for b in range(BOOKS):
                cd = codes[b, at, cols]
                lo = lax.shift_right_logical(cd, HBITS).astype(f32)
                hi = lax.bitwise_and(cd, HIGH - 1).astype(f32)
                a, o = [], []
                for g in range(unroll):
                    sg = s[8 * g : 8 * g + 8]
                    two = jnp.concatenate([sg, sg], axis=0).astype(bf16)
                    lo_b = jnp.broadcast_to(lo[g : g + 1], (16, LANES)).astype(bf16)
                    a.append(jnp.concatenate([jnp.where(lo_b == r, two, zero16) for r in row_low], axis=0))
                    hi_b = jnp.broadcast_to(hi[g : g + 1], (16, LANES)).astype(bf16)
                    o.append(jnp.concatenate([jnp.where(hi_b == r, one16, zero16) for r in row_high], axis=0))
                left_m = jnp.concatenate(a, axis=1)
                right_m = jnp.concatenate(o, axis=1)
                hloc[b] += lax.dot_general(
                    right_m, left_m, (((1,), (1,)), ((), ())), preferred_element_type=f32
                )

    for n, (src, dst) in enumerate(operands):
        pltpu.make_async_copy(src, dst, loc_sem.at[nc + 1 + n]).wait()
    for b in range(BOOKS):
        table[b] = books[b].astype(bf16).astype(f32)
    todo = []

    def add(at, job, *args):
        todo.append((at, functools.partial(job, *args)))

    def sides(r):
        pairs = []
        if r == 0:
            pairs.append((lambda: iz, 0))
        else:
            pairs.append((lambda: left_of(r), 2 * r - 1))
            if r < half:
                pairs.append((lambda: right_of(r), 2 * r))
        return pairs

    def on_sides(job, r):
        for block, slot in sides(r):
            job(block(), slot)

    def one_side(job, r, n):
        block, slot = sides(r)[n]
        job(block(), slot)

    for c in range(nc):
        add((0, 0, 1, 1, 1, 2, 2)[c], decode, c)
    for k in range(1, chips):
        add(3, x_forward, k)
    for k in range(chips):
        add(4, x_ready, k)
    when_early = (2, 3, 3, 4, 5, 6, 7, 8, 9)
    when_late = (3, 3, 4, 5, 6, 7, 8, 9, 10)
    for r in range(half + 1):
        for n in range(len(sides(r))):
            add(when_early[r], one_side, g_early, r, n)
    for r in range(half):
        add(when_late[r] + 1, on_sides, g_pass, r)
    for r in range(half + 1):
        for n in range(len(sides(r))):
            add(when_late[r], one_side, g_late, r, n)
    for q in range(half):
        add((5, 5, 5, 6, 6, 7, 8, 9)[q], gw_pair, q, early)
    for q in range(half):
        add((5, 5, 6, 6, 7, 8, 9, 10)[q], gw_pair, q, late)
    for at, job in todo:
        if at == 0:
            job()
    last = half + skew
    for v in range(1, last + 1):
        ops = []
        if v <= half:
            ops += [functools.partial(ring, v, c) for c in early]
        if 1 <= v - skew <= half:
            ops += [functools.partial(ring, v - skew, c) for c in late]
        jobs = [job for at, job in todo if at == v]
        slots = len(ops)
        for n, op in enumerate(ops):
            op()
            for job in jobs[n * len(jobs) // slots : (n + 1) * len(jobs) // slots]:
                job()
    for at, job in todo:
        if at == last + 1:
            job()
    for n, c in enumerate(early + late):
        finish(c)
        if n == 0:
            g_pass(left_of(half), 2 * half - 1)

    def s_copy(k):
        dev = lax.rem(iz + k, nz)
        return remote(sown, sz.at[iz], s_send.at[k - 1], s_recv.at[iz], din=dev)

    for k in range(1, nz):
        s_copy(k).start()

    pieces = hfin.shape[0]
    mine = lax.rem(jd, pieces)
    for b in range(BOOKS):
        turned = jnp.transpose(hloc[b])
        for h in range(2):
            part = jnp.concatenate(
                [turned[8 * n : 8 * n + 8, :] for n in range(LOW // 2 * h, LOW // 2 * (h + 1))], axis=1
            )
            hbk[4 * b + 2 * h] = part[0:4]
            hbk[4 * b + 2 * h + 1] = part[4:8]

    def h_copy(k):
        other = lax.rem(jd + k, nd)
        return remote(
            hbk.at[lax.rem(other, pieces)], hplane.at[jd], hx_send.at[k - 1], hx_recv.at[jd], dout=other
        )

    for k in range(1, nd):
        h_copy(k).start()
    hplane[jd] = hbk[mine]
    for k in range(1, nd):
        src = lax.rem(jd + nd - k, nd)
        remote(hbk.at[0], hplane.at[src], hx_send.at[0], hx_recv.at[src], dout=src).wait_recv()
    hz[iz] = jnp.sum(hplane[...], axis=0)

    def z_copy(k):
        dev = lax.rem(iz + k, nz)
        return remote(hz.at[iz], hz.at[iz], hz_send.at[k - 1], hz_recv.at[iz], din=dev)

    for k in range(1, nz):
        z_copy(k).start()

    sz[iz] = sown[...]
    for k in range(1, nz):
        src = lax.rem(iz + nz - k, nz)
        remote(sown, sz.at[src], s_send.at[0], s_recv.at[src], din=src).wait_recv()
    scale_out[...] = jnp.sum(sz[...], axis=0)

    for k in range(1, chips):
        src = lax.rem(chip + chips - k, chips)
        remote(rss.at[0], rsr.at[src], r_send.at[0], r_recv.at[src], dout=2 * src + core).wait_recv()
    slot_own = 0
    dist = lax.rem(chip - iz + nz, nz)
    slot_own = jnp.where(dist == 0, 0, jnp.where(dist < half, 2 * dist, 2 * (nz - dist) - 1))
    pltpu.make_async_copy(rss.at[slot_own], rsr.at[chip], r_send.at[slot_own]).wait()
    acc = rsr[0].astype(f32)
    for k in range(1, chips):
        acc = acc + rsr[k].astype(f32)
    gx_out[...] = acc.astype(bf16)

    for k in range(1, nz):
        src = lax.rem(iz + nz - k, nz)
        remote(hz.at[src], hz.at[src], hz_send.at[0], hz_recv.at[src], din=src).wait_recv()
    hfin[mine] = jnp.sum(hz[...], axis=0)

    def f_copy(k):
        dev = jd - mine + lax.rem(mine + k, pieces)
        return remote(hfin.at[mine], hfin.at[mine], hf_send.at[k - 1], hf_recv.at[mine], dout=dev)

    for k in range(1, pieces):
        f_copy(k).start()
    for k in range(1, pieces):
        src = lax.rem(mine + k, pieces)
        remote(hfin.at[src], hfin.at[src], hf_send.at[0], hf_recv.at[src], dout=mate).wait_recv()
    for b in range(BOOKS):
        for h in range(2):
            book_out[b, :, pl.ds(h * LANES, LANES)] = jnp.concatenate(
                [hfin[4 * b + 2 * h], hfin[4 * b + 2 * h + 1]], axis=0
            )

    for s in range(half):
        wr = gyf.at[pl.ds(0, nc if s < half - 1 else n_right), rows_of(left_of(s))]
        remote(wr, wr, gy_send.at[0, s], gy_recv.at[0, s, 0], din=right).wait_send()
        if s < half - 1:
            wl = gyf.at[:, rows_of(right_of(s))]
        else:
            wl = gyf.at[pl.ds(0, nc - n_right), rows_of(right_of(s))]
        if s < half - 1 or nc > n_right:
            remote(wl, wl, gy_send.at[1, s], gy_recv.at[1, s, 0], din=left).wait_send()
    for k in range(2 * chips - 1):
        x_copy(jd, mate, k).wait_send()
    for k in range(1, nz):
        s_copy(k).wait_send()
        z_copy(k).wait_send()
    for k in range(1, nd):
        h_copy(k).wait_send()
    for k in range(1, pieces):
        f_copy(k).wait_send()
    for k in range(nz):
        remote(gst.at[k, 1 - core], gpr.at[k], p_send.at[k], p_recv.at[k], dout=mate).wait_send()

        @pl.when(k != slot_own)
        def _():
            remote(rss.at[k], rsr.at[chip], r_send.at[k], r_recv.at[chip], dout=mate).wait_send()


def fused(nz, nd, x, gy, codes, books, scales):
    xrows, feats = x.shape
    rows, outs = gy.shape
    nc = outs // LANES
    chips = nd // 2
    half = nz // 2
    bf16, f32 = jnp.bfloat16, jnp.float32
    V = pltpu.VMEM
    D = pltpu.SemaphoreType.DMA
    vm = pl.BlockSpec(memory_space=pltpu.VMEM)
    anyspec = pl.BlockSpec(memory_space=pl.ANY)
    tile = (GROUP // 2, LANES)
    scratch = [
        V(codes.shape, jnp.int32),
        V(books.shape, f32),
        V(scales.shape, f32),
        V((nc, rows * nz, LANES), bf16),
        V((nd, xrows, feats), bf16),
        V((nz, feats, rows), bf16),
        V((feats, outs), bf16),
        V((feats, outs), f32),
        V((feats, outs), f32),
        V((BOOKS, GROUP, KCODE), f32),
        V((nz, 2, rows // 2, feats), f32),
        V((nz, 2, rows // 2, feats), bf16),
        V((nz, rows // 2, feats), bf16),
        V((nz, rows // 2, feats), bf16),
        V((chips, rows // 2, feats), bf16),
        V((BOOKS, HIGH, LOW * 8), f32),
        V((8,) + tile, f32),
        V((nd,) + tile, f32),
        V((nz,) + tile, f32),
        V((8,) + tile, f32),
        V((8, LANES), f32),
        V((nz, 8, LANES), f32),
        D((nc + 4,)),
        D((2, half)),
        D((2, half, nc)),
        D((2 * chips - 1,)),
        D((nd,)),
        D((nz,)),
        D((nz,)),
        D((nz,)),
        D((chips,)),
        D((nd,)),
        D((nd,)),
        D((nz,)),
        D((nz,)),
        D((8,)),
        D((8,)),
        D((nz,)),
        D((nz,)),
    ]
    return pl.pallas_call(
        functools.partial(kernel, nz, nd),
        out_shape=(
            jax.ShapeDtypeStruct((xrows, feats), bf16),
            jax.ShapeDtypeStruct((BOOKS, GROUP, KCODE), f32),
            jax.ShapeDtypeStruct((8, LANES), f32),
        ),
        in_specs=[anyspec] * 5,
        out_specs=(vm, vm, vm),
        scratch_shapes=scratch,
        compiler_params=pltpu.CompilerParams(
            collective_id=0, has_side_effects=True, vmem_limit_bytes=60 * 1024 * 1024
        ),
        name="fused",
    )(x, gy, codes, books, scales)


def local(nz, nd, inputs, cotangent, codes, codebooks, scales, book_mean, book_var, scale_mean, scale_var):
    norm_factor = 1.0 / (2.0 * DOUT) ** 0.5
    loss_scale = (TOKENS * DIN / 4096.0) ** 0.5
    outs = scales.shape[0]
    gx, book, scale = fused(nz, nd, inputs, cotangent, codes, jnp.transpose(codebooks, (0, 2, 1)), scales)
    book_grad = jnp.transpose(book, (0, 2, 1)) / loss_scale
    scale_grad = scale[: outs // LANES].reshape(outs) * norm_factor / loss_scale
    new_books, new_book_mean, new_book_var = adam_step(codebooks, book_mean, book_var, book_grad)
    new_scales, new_scale_mean, new_scale_var = adam_step(scales, scale_mean, scale_var, scale_grad)
    return (
        gx,
        book_grad,
        new_books,
        new_book_mean,
        new_book_var,
        new_scales,
        new_scale_mean,
        new_scale_var,
    )


def solution(mesh):
    nz, nd = mesh.shape["din"], mesh.shape["dout"]
    in_specs = (
        P("dout", "din"),
        P("din", "dout"),
        P(None, "din", "dout"),
        P(),
        P("dout"),
        P(),
        P(),
        P("dout"),
        P("dout"),
    )
    out_specs = (P("dout", "din"), P(), P(), P(), P(), P("dout"), P("dout"), P("dout"))
    return jax.shard_map(
        functools.partial(local, nz, nd), mesh=mesh, in_specs=in_specs, out_specs=out_specs, check_vma=False
    )
```

```python
import functools

import jax
import jax.numpy as jnp
from jax import lax
from jax.experimental import pallas as pl
from jax.experimental.pallas import tpu as pltpu
from jax.sharding import PartitionSpec as P

DIN = 8192
DOUT = 28672
KCODE = 256
BOOKS = 2
GROUP = 8
TOKENS = 2048

beta_one = 0.9
beta_two = 0.999
adam_rate = 0.01
adam_eps = 1e-08
corr_one = 1.0 - 0.9**10
corr_two = 1.0 - 0.999**10

LANES = 128
LOW = 8
HBITS = 5
SKEW = 1
UNROLL = 16
HIGH = KCODE // LOW


def adam_step(param, mean_old, var_old, gradient):
    mean_new = beta_one * mean_old + (1.0 - beta_one) * gradient
    var_new = beta_two * var_old + (1.0 - beta_two) * gradient * gradient
    update = mean_new / corr_one / (jnp.sqrt(var_new / corr_two) + adam_eps)
    return (param - adam_rate * update, mean_new, var_new)


def kernel(
    nz, nd, x_hbm, gy_hbm, codes_hbm, books_hbm, scales_hbm, gx_out, book_out, scale_out,
    codes, books, scales, gyf, xf, xt, wts, dec, gw, table, gkeep, gst, gpr, rss, rsr, hloc, hbk, hplane, hz, hfin, sown, sz,
    loc_sem, gy_send, gy_recv, x_send, x_recv, p_send, p_recv, r_send, r_recv,
    hx_send, hx_recv, hz_send, hz_recv, hf_send, hf_recv, s_send, s_recv,
):
    chips = nd // 2
    half = nz // 2
    nc = gyf.shape[0]
    early = list(range((nc + 1) // 2))
    late = list(range((nc + 1) // 2, nc))
    goes_right = [k % 2 == 0 for k in range(nc)]
    n_right = sum(goes_right)
    skew = min(SKEW, half - 1)
    rows = gy_hbm.shape[0]
    xrows = x_hbm.shape[0]
    feats = x_hbm.shape[1]
    groups = codes.shape[1]
    iz = lax.axis_index("din")
    jd = lax.axis_index("dout")
    chip = jd // 2
    core = jd % 2
    mate = jd + 1 - 2 * core
    right = lax.rem(iz + 1, nz)
    left = lax.rem(iz + nz - 1, nz)
    f32 = jnp.float32
    bf16 = jnp.bfloat16

    def remote(src, dst, ssem, rsem, din=None, dout=None):
        where = {}
        if din is not None:
            where["din"] = din
        if dout is not None:
            where["dout"] = dout
        return pltpu.make_async_remote_copy(
            src_ref=src, dst_ref=dst, send_sem=ssem, recv_sem=rsem,
            device_id=where, device_id_type=pl.DeviceIdType.MESH,
        )

    def rows_of(block):
        return pl.ds(pl.multiple_of(block * rows, rows), rows)

    barrier = pltpu.get_barrier_semaphore()
    for dev in (right, left):
        pl.semaphore_signal(barrier, 1, device_id={"din": dev}, device_id_type=pl.DeviceIdType.MESH)
    for k in range(1, nd):
        pl.semaphore_signal(barrier, 1, device_id={"dout": lax.rem(jd + k, nd)}, device_id_type=pl.DeviceIdType.MESH)

    for c in range(nc):
        pltpu.make_async_copy(
            gy_hbm.at[:, pl.ds(c * LANES, LANES)], gyf.at[c, rows_of(iz)], loc_sem.at[c]
        ).start()
    pltpu.make_async_copy(x_hbm, xf.at[jd], loc_sem.at[nc]).start()
    operands = ((codes_hbm, codes), (books_hbm, books), (scales_hbm, scales))
    for n, (src, dst) in enumerate(operands):
        pltpu.make_async_copy(src, dst, loc_sem.at[nc + 1 + n]).start()

    norm_factor = 1.0 / (2.0 * DOUT) ** 0.5
    def coef_of(c):
        return scales[pl.ds(c * LANES, LANES)].reshape(1, LANES) * norm_factor

    def lookup(which, idx):
        low = lax.bitwise_and(idx, LANES - 1)
        first = jnp.take_along_axis(table[which, :, 0:LANES], low, axis=1, mode="promise_in_bounds")
        second = jnp.take_along_axis(table[which, :, LANES:KCODE], low, axis=1, mode="promise_in_bounds")
        return jnp.where(idx >= LANES, second, first)

    unroll = min(UNROLL, groups)

    def decode(c):
        cols = pl.ds(c * LANES, LANES)
        co = coef_of(c)

        @pl.loop(0, groups // unroll)
        def _(q):
            at = pl.ds(pl.multiple_of(q * unroll, unroll), unroll)
            c0 = codes[0, at, cols]
            c1 = codes[1, at, cols]
            out = []
            for g in range(unroll):
                d = lookup(0, jnp.broadcast_to(c0[g : g + 1], (8, LANES))) + lookup(
                    1, jnp.broadcast_to(c1[g : g + 1], (8, LANES))
                )
                out.append(d)
            d = jnp.concatenate(out, axis=0)
            where = pl.ds(pl.multiple_of(q * unroll * 8, unroll * 8), unroll * 8)
            dec[where, cols] = d
            wts[where, cols] = (d * co).astype(bf16)

    for c in range(nc):
        pltpu.make_async_copy(
            gy_hbm.at[:, pl.ds(c * LANES, LANES)], gyf.at[c, rows_of(iz)], loc_sem.at[c]
        ).wait()
    pltpu.make_async_copy(x_hbm, xf.at[jd], loc_sem.at[nc]).wait()
    pl.semaphore_wait(barrier, 2 + nd - 1)

    def send_right(s, c):
        block = lax.rem(iz - s + nz, nz)
        part = gyf.at[c, rows_of(block)]
        return remote(part, part, gy_send.at[0, s], gy_recv.at[0, s, c], din=right)

    def send_left(s, c):
        block = lax.rem(iz + s, nz)
        part = gyf.at[c, rows_of(block)]
        return remote(part, part, gy_send.at[1, s], gy_recv.at[1, s, c], din=left)

    def send_own(c):
        if half > 1 or goes_right[c]:
            send_right(0, c).start()
        if half > 1 or not goes_right[c]:
            send_left(0, c).start()

    for c in range(nc):
        send_own(c)

    def x_copy(k, dev, sem):
        return remote(xf.at[k], xf.at[k], x_send.at[sem], x_recv.at[k], dout=dev)

    x_copy(jd, mate, 2 * chips - 2).start()
    for k in range(1, chips):
        x_copy(jd, 2 * lax.rem(chip + k, chips) + core, k - 1).start()

    def x_forward(k):
        src = 2 * lax.rem(chip + chips - k, chips) + core
        x_copy(src, mate, chips - 1 + k - 1).wait_recv()
        x_copy(src, mate, chips - 1 + k - 1).start()

    def ring(r, c):
        bl = lax.rem(iz - r + nz, nz)
        br = lax.rem(iz + r, nz)
        if r < half or goes_right[c]:
            part = gyf.at[c, rows_of(bl)]
            remote(part, part, gy_send.at[0, 0], gy_recv.at[0, r - 1, c], din=right).wait_recv()
            if r < half - 1 or (r == half - 1 and goes_right[c]):
                send_right(r, c).start()
        if r < half or not goes_right[c]:
            part = gyf.at[c, rows_of(br)]
            remote(part, part, gy_send.at[1, 0], gy_recv.at[1, r - 1, c], din=left).wait_recv()
            if r < half - 1 or (r == half - 1 and not goes_right[c]):
                send_left(r, c).start()

    def g_dot(block, chunks):
        lhs = jnp.concatenate([gyf[c, rows_of(block)] for c in chunks], axis=1)
        rhs = wts[:, pl.ds(chunks[0] * LANES, len(chunks) * LANES)]
        return lax.dot_general(lhs, rhs, (((1,), (1,)), ((), ())), preferred_element_type=f32)

    def g_early(block, slot):
        gkeep[slot] = g_dot(block, early).reshape(2, rows // 2, feats)

    def g_late(block, slot):
        g = gkeep[slot] + g_dot(block, late).reshape(2, rows // 2, feats)
        gkeep[slot] = g
        gst[slot] = g.astype(bf16)
        remote(gst.at[slot, 1 - core], gpr.at[slot], p_send.at[slot], p_recv.at[slot], dout=mate).start()

    def g_pass(block, slot):
        remote(gst.at[slot, 1 - core], gpr.at[slot], p_send.at[slot], p_recv.at[slot], dout=mate).wait_recv()
        total = gkeep[slot, core] + gpr[slot].astype(f32)
        rss[slot] = total.astype(bf16)

        @pl.when(block == chip)
        def _():
            pltpu.make_async_copy(rss.at[slot], rsr.at[chip], r_send.at[slot]).start()

        @pl.when(block != chip)
        def _():
            remote(rss.at[slot], rsr.at[chip], r_send.at[slot], r_recv.at[chip], dout=2 * block + core).start()

    def left_of(r):
        return lax.rem(iz - r + nz, nz)

    def right_of(r):
        return lax.rem(iz + r, nz)

    def gw_pair(q, chunks):
        b0, b1 = right_of(q), left_of(q + 1)
        lhs = jnp.concatenate([xt[b0], xt[b1]], axis=1)
        for c in chunks:
            rhs = jnp.concatenate([gyf[c, rows_of(b0)], gyf[c, rows_of(b1)]], axis=0)
            d = jnp.dot(lhs, rhs, preferred_element_type=f32)
            cols = pl.ds(c * LANES, LANES)
            if q == 0:
                gw[:, cols] = d
            else:
                gw[:, cols] += d

    def transpose_x(k):
        blk = xf[pl.ds(2 * k, 2)].reshape(rows, feats)
        xt[k] = jnp.transpose(blk)

    def x_ready(k):
        src = 2 * k + 1 - core
        x_copy(src, mate, 0).wait_recv()
        transpose_x(k)

    hloc[...] = jnp.zeros_like(hloc)
    sown[...] = jnp.zeros_like(sown)
    rows16 = lax.broadcasted_iota(jnp.int32, (16, LANES), 0)
    row_low = [(rows16 // 8 + 2 * n).astype(f32).astype(bf16) for n in range(LOW // 2)]
    row_high = [(rows16 + 16 * n).astype(f32).astype(bf16) for n in range(HIGH // 16)]
    zero16 = jnp.zeros((16, LANES), bf16)
    one16 = jnp.ones((16, LANES), bf16)

    def scale_part(c):
        cols = pl.ds(c * LANES, LANES)
        sown[c : c + 1, :] = jnp.sum(dec[:, cols] * gw[:, cols], axis=0, keepdims=True)

    def piece(c, q):
        cols = pl.ds(c * LANES, LANES)
        co = coef_of(c)
        if True:
            at = pl.ds(pl.multiple_of(q * unroll, unroll), unroll)
            s = gw[pl.ds(pl.multiple_of(q * unroll * 8, unroll * 8), unroll * 8), cols] * co
            for b in range(BOOKS):
                cd = codes[b, at, cols]
                lo = lax.shift_right_logical(cd, HBITS).astype(f32)
                hi = lax.bitwise_and(cd, HIGH - 1).astype(f32)
                a, o = [], []
                for g in range(unroll):
                    sg = s[8 * g : 8 * g + 8]
                    two = jnp.concatenate([sg, sg], axis=0).astype(bf16)
                    lo_b = jnp.broadcast_to(lo[g : g + 1], (16, LANES)).astype(bf16)
                    a.append(jnp.concatenate([jnp.where(lo_b == r, two, zero16) for r in row_low], axis=0))
                    hi_b = jnp.broadcast_to(hi[g : g + 1], (16, LANES)).astype(bf16)
                    o.append(jnp.concatenate([jnp.where(hi_b == r, one16, zero16) for r in row_high], axis=0))
                left_m = jnp.concatenate(a, axis=1)
                right_m = jnp.concatenate(o, axis=1)
                hloc[b] += lax.dot_general(
                    right_m, left_m, (((1,), (1,)), ((), ())), preferred_element_type=f32
                )

    def finish(c):
        scale_part(c)

        @pl.loop(0, groups // unroll)
        def _(q):
            piece(c, q)

    for n, (src, dst) in enumerate(operands):
        pltpu.make_async_copy(src, dst, loc_sem.at[nc + 1 + n]).wait()
    for b in range(BOOKS):
        table[b] = books[b].astype(bf16).astype(f32)
    todo = []

    def add(at, job, *args):
        todo.append((at, functools.partial(job, *args)))

    def sides(r):
        pairs = []
        if r == 0:
            pairs.append((lambda: iz, 0))
        else:
            pairs.append((lambda: left_of(r), 2 * r - 1))
            if r < half:
                pairs.append((lambda: right_of(r), 2 * r))
        return pairs

    def on_sides(job, r):
        for block, slot in sides(r):
            job(block(), slot)

    def one_side(job, r, n):
        block, slot = sides(r)[n]
        job(block(), slot)

    for c in range(nc):
        add((0, 0, 1, 1, 1, 2, 2)[c], decode, c)
    for k in range(1, chips):
        add(3, x_forward, k)
    for k in range(chips):
        add(4, x_ready, k)
    when_early = (2, 3, 3, 4, 5, 6, 7, 8, 9)
    when_late = (3, 3, 4, 5, 6, 7, 8, 9, 10)
    for r in range(half + 1):
        for n in range(len(sides(r))):
            add(when_early[r], one_side, g_early, r, n)
    for r in range(half - 1):
        add(when_late[r] + 1, on_sides, g_pass, r)
    for r in range(half + 1):
        for n in range(len(sides(r))):
            add(when_late[r], one_side, g_late, r, n)
    for q in range(half):
        add((5, 5, 5, 6, 6, 7, 8, 9)[q], gw_pair, q, early)
    for q in range(half):
        add((5, 5, 6, 6, 7, 8, 9, 10)[q], gw_pair, q, late)
    for at, job in todo:
        if at == 0:
            job()
    last = half + skew
    for v in range(1, last + 1):
        ops = []
        if v <= half:
            ops += [functools.partial(ring, v, c) for c in early]
        if 1 <= v - skew <= half:
            ops += [functools.partial(ring, v - skew, c) for c in late]
        jobs = [job for at, job in todo if at == v]
        slots = len(ops)
        for n, op in enumerate(ops):
            op()
            for job in jobs[n * len(jobs) // slots : (n + 1) * len(jobs) // slots]:
                job()
    for at, job in todo:
        if at == last + 1:
            job()
    for n, c in enumerate(early + late):
        finish(c)
        if n == 0:
            on_sides(g_pass, half - 1)
        if n == 1:
            g_pass(left_of(half), 2 * half - 1)

    def s_copy(k):
        dev = lax.rem(iz + k, nz)
        return remote(sown, sz.at[iz], s_send.at[k - 1], s_recv.at[iz], din=dev)

    for k in range(1, nz):
        s_copy(k).start()

    pieces = hfin.shape[0]
    mine = lax.rem(jd, pieces)
    for b in range(BOOKS):
        turned = jnp.transpose(hloc[b])
        for h in range(2):
            part = jnp.concatenate(
                [turned[8 * n : 8 * n + 8, :] for n in range(LOW // 2 * h, LOW // 2 * (h + 1))], axis=1
            )
            hbk[4 * b + 2 * h] = part[0:4]
            hbk[4 * b + 2 * h + 1] = part[4:8]

    def h_copy(k):
        other = lax.rem(jd + k, nd)
        return remote(
            hbk.at[lax.rem(other, pieces)], hplane.at[jd], hx_send.at[k - 1], hx_recv.at[jd], dout=other
        )

    for k in range(1, nd):
        h_copy(k).start()
    hplane[jd] = hbk[mine]
    for k in range(1, nd):
        src = lax.rem(jd + nd - k, nd)
        remote(hbk.at[0], hplane.at[src], hx_send.at[0], hx_recv.at[src], dout=src).wait_recv()
    hz[iz] = jnp.sum(hplane[...], axis=0)

    def z_copy(k):
        dev = lax.rem(iz + k, nz)
        return remote(hz.at[iz], hz.at[iz], hz_send.at[k - 1], hz_recv.at[iz], din=dev)

    for k in range(1, nz):
        z_copy(k).start()

    sz[iz] = sown[...]
    for k in range(1, nz):
        src = lax.rem(iz + nz - k, nz)
        remote(sown, sz.at[src], s_send.at[0], s_recv.at[src], din=src).wait_recv()
    scale_out[...] = jnp.sum(sz[...], axis=0)

    for k in range(1, chips):
        src = lax.rem(chip + chips - k, chips)
        remote(rss.at[0], rsr.at[src], r_send.at[0], r_recv.at[src], dout=2 * src + core).wait_recv()
    slot_own = 0
    dist = lax.rem(chip - iz + nz, nz)
    slot_own = jnp.where(dist == 0, 0, jnp.where(dist < half, 2 * dist, 2 * (nz - dist) - 1))
    pltpu.make_async_copy(rss.at[slot_own], rsr.at[chip], r_send.at[slot_own]).wait()
    acc = rsr[0].astype(f32)
    for k in range(1, chips):
        acc = acc + rsr[k].astype(f32)
    gx_out[...] = acc.astype(bf16)

    for k in range(1, nz):
        src = lax.rem(iz + nz - k, nz)
        remote(hz.at[src], hz.at[src], hz_send.at[0], hz_recv.at[src], din=src).wait_recv()
    hfin[mine] = jnp.sum(hz[...], axis=0)

    def f_copy(k):
        dev = jd - mine + lax.rem(mine + k, pieces)
        return remote(hfin.at[mine], hfin.at[mine], hf_send.at[k - 1], hf_recv.at[mine], dout=dev)

    for k in range(1, pieces):
        f_copy(k).start()
    for k in range(1, pieces):
        src = lax.rem(mine + k, pieces)
        remote(hfin.at[src], hfin.at[src], hf_send.at[0], hf_recv.at[src], dout=mate).wait_recv()
    for b in range(BOOKS):
        for h in range(2):
            book_out[b, :, pl.ds(h * LANES, LANES)] = jnp.concatenate(
                [hfin[4 * b + 2 * h], hfin[4 * b + 2 * h + 1]], axis=0
            )

    for s in range(half):
        wr = gyf.at[pl.ds(0, nc if s < half - 1 else n_right), rows_of(left_of(s))]
        remote(wr, wr, gy_send.at[0, s], gy_recv.at[0, s, 0], din=right).wait_send()
        if s < half - 1:
            wl = gyf.at[:, rows_of(right_of(s))]
        else:
            wl = gyf.at[pl.ds(0, nc - n_right), rows_of(right_of(s))]
        if s < half - 1 or nc > n_right:
            remote(wl, wl, gy_send.at[1, s], gy_recv.at[1, s, 0], din=left).wait_send()
    for k in range(2 * chips - 1):
        x_copy(jd, mate, k).wait_send()
    for k in range(1, nz):
        s_copy(k).wait_send()
        z_copy(k).wait_send()
    for k in range(1, nd):
        h_copy(k).wait_send()
    for k in range(1, pieces):
        f_copy(k).wait_send()
    for k in range(nz):
        remote(gst.at[k, 1 - core], gpr.at[k], p_send.at[k], p_recv.at[k], dout=mate).wait_send()

        @pl.when(k != slot_own)
        def _():
            remote(rss.at[k], rsr.at[chip], r_send.at[k], r_recv.at[chip], dout=mate).wait_send()


def fused(nz, nd, x, gy, codes, books, scales):
    xrows, feats = x.shape
    rows, outs = gy.shape
    nc = outs // LANES
    chips = nd // 2
    half = nz // 2
    bf16, f32 = jnp.bfloat16, jnp.float32
    V = pltpu.VMEM
    D = pltpu.SemaphoreType.DMA
    vm = pl.BlockSpec(memory_space=pltpu.VMEM)
    anyspec = pl.BlockSpec(memory_space=pl.ANY)
    tile = (GROUP // 2, LANES)
    scratch = [
        V(codes.shape, jnp.int32),
        V(books.shape, f32),
        V(scales.shape, f32),
        V((nc, rows * nz, LANES), bf16),
        V((nd, xrows, feats), bf16),
        V((nz, feats, rows), bf16),
        V((feats, outs), bf16),
        V((feats, outs), f32),
        V((feats, outs), f32),
        V((BOOKS, GROUP, KCODE), f32),
        V((nz, 2, rows // 2, feats), f32),
        V((nz, 2, rows // 2, feats), bf16),
        V((nz, rows // 2, feats), bf16),
        V((nz, rows // 2, feats), bf16),
        V((chips, rows // 2, feats), bf16),
        V((BOOKS, HIGH, LOW * 8), f32),
        V((8,) + tile, f32),
        V((nd,) + tile, f32),
        V((nz,) + tile, f32),
        V((8,) + tile, f32),
        V((8, LANES), f32),
        V((nz, 8, LANES), f32),
        D((nc + 4,)),
        D((2, half)),
        D((2, half, nc)),
        D((2 * chips - 1,)),
        D((nd,)),
        D((nz,)),
        D((nz,)),
        D((nz,)),
        D((chips,)),
        D((nd,)),
        D((nd,)),
        D((nz,)),
        D((nz,)),
        D((8,)),
        D((8,)),
        D((nz,)),
        D((nz,)),
    ]
    return pl.pallas_call(
        functools.partial(kernel, nz, nd),
        out_shape=(
            jax.ShapeDtypeStruct((xrows, feats), bf16),
            jax.ShapeDtypeStruct((BOOKS, GROUP, KCODE), f32),
            jax.ShapeDtypeStruct((8, LANES), f32),
        ),
        in_specs=[anyspec] * 5,
        out_specs=(vm, vm, vm),
        scratch_shapes=scratch,
        compiler_params=pltpu.CompilerParams(
            collective_id=0, has_side_effects=True, vmem_limit_bytes=60 * 1024 * 1024
        ),
        name="fused",
    )(x, gy, codes, books, scales)


def local(nz, nd, inputs, cotangent, codes, codebooks, scales, book_mean, book_var, scale_mean, scale_var):
    norm_factor = 1.0 / (2.0 * DOUT) ** 0.5
    loss_scale = (TOKENS * DIN / 4096.0) ** 0.5
    outs = scales.shape[0]
    gx, book, scale = fused(nz, nd, inputs, cotangent, codes, jnp.transpose(codebooks, (0, 2, 1)), scales)
    book_grad = jnp.transpose(book, (0, 2, 1)) / loss_scale
    scale_grad = scale[: outs // LANES].reshape(outs) * norm_factor / loss_scale
    new_books, new_book_mean, new_book_var = adam_step(codebooks, book_mean, book_var, book_grad)
    new_scales, new_scale_mean, new_scale_var = adam_step(scales, scale_mean, scale_var, scale_grad)
    return (
        gx,
        book_grad,
        new_books,
        new_book_mean,
        new_book_var,
        new_scales,
        new_scale_mean,
        new_scale_var,
    )


def solution(mesh):
    nz, nd = mesh.shape["din"], mesh.shape["dout"]
    in_specs = (
        P("dout", "din"),
        P("din", "dout"),
        P(None, "din", "dout"),
        P(),
        P("dout"),
        P(),
        P(),
        P("dout"),
        P("dout"),
    )
    out_specs = (P("dout", "din"), P(), P(), P(), P(), P("dout"), P("dout"), P("dout"))
    return jax.shard_map(
        functools.partial(local, nz, nd), mesh=mesh, in_specs=in_specs, out_specs=out_specs, check_vma=False
    )
```

```python
import functools

import jax
import jax.numpy as jnp
from jax import lax
from jax.experimental import pallas as pl
from jax.experimental.pallas import tpu as pltpu
from jax.sharding import PartitionSpec as P

DIN = 8192
DOUT = 28672
KCODE = 256
BOOKS = 2
GROUP = 8
TOKENS = 2048

beta_one = 0.9
beta_two = 0.999
adam_rate = 0.01
adam_eps = 1e-08
corr_one = 1.0 - 0.9**10
corr_two = 1.0 - 0.999**10

LANES = 128
LOW = 8
HBITS = 5
SKEW = 2
UNROLL = 16
HIGH = KCODE // LOW


def adam_step(param, mean_old, var_old, gradient):
    mean_new = beta_one * mean_old + (1.0 - beta_one) * gradient
    var_new = beta_two * var_old + (1.0 - beta_two) * gradient * gradient
    update = mean_new / corr_one / (jnp.sqrt(var_new / corr_two) + adam_eps)
    return (param - adam_rate * update, mean_new, var_new)


def kernel(
    nz, nd, x_hbm, gy_hbm, codes_hbm, books_hbm, scales_hbm, gx_out, book_out, scale_out,
    codes, books, scales, gyf, xf, xt, wts, dec, gw, table, gkeep, gst, gpr, rss, rsx, rsy, rsr, hloc, hbk, hplane, hz, hfin, sown, sz,
    loc_sem, gy_send, gy_recv, x_send, x_recv, p_send, p_recv, r_send, r_recv, y_send, y_recv,
    hx_send, hx_recv, hz_send, hz_recv, hf_send, hf_recv, s_send, s_recv,
):
    chips = nd // 2
    half = nz // 2
    nc = gyf.shape[0]
    early = list(range((nc + 1) // 2))
    late = list(range((nc + 1) // 2, nc))
    goes_right = [k % 2 == 0 for k in range(nc)]
    n_right = sum(goes_right)
    skew = min(SKEW, half - 1)
    rows = gy_hbm.shape[0]
    xrows = x_hbm.shape[0]
    feats = x_hbm.shape[1]
    groups = codes.shape[1]
    iz = lax.axis_index("din")
    jd = lax.axis_index("dout")
    chip = jd // 2
    core = jd % 2
    mate = jd + 1 - 2 * core
    across = rsx.shape[1]
    my_y, my_x = chip // across, lax.rem(chip, across)
    right = lax.rem(iz + 1, nz)
    left = lax.rem(iz + nz - 1, nz)
    f32 = jnp.float32
    bf16 = jnp.bfloat16

    def remote(src, dst, ssem, rsem, din=None, dout=None):
        where = {}
        if din is not None:
            where["din"] = din
        if dout is not None:
            where["dout"] = dout
        return pltpu.make_async_remote_copy(
            src_ref=src, dst_ref=dst, send_sem=ssem, recv_sem=rsem,
            device_id=where, device_id_type=pl.DeviceIdType.MESH,
        )

    def rows_of(block):
        return pl.ds(pl.multiple_of(block * rows, rows), rows)

    barrier = pltpu.get_barrier_semaphore()
    for dev in (right, left):
        pl.semaphore_signal(barrier, 1, device_id={"din": dev}, device_id_type=pl.DeviceIdType.MESH)
    for k in range(1, nd):
        pl.semaphore_signal(barrier, 1, device_id={"dout": lax.rem(jd + k, nd)}, device_id_type=pl.DeviceIdType.MESH)

    for c in range(nc):
        pltpu.make_async_copy(
            gy_hbm.at[:, pl.ds(c * LANES, LANES)], gyf.at[c, rows_of(iz)], loc_sem.at[c]
        ).start()
    pltpu.make_async_copy(x_hbm, xf.at[jd], loc_sem.at[nc]).start()
    operands = ((codes_hbm, codes), (books_hbm, books), (scales_hbm, scales))
    for n, (src, dst) in enumerate(operands):
        pltpu.make_async_copy(src, dst, loc_sem.at[nc + 1 + n]).start()

    norm_factor = 1.0 / (2.0 * DOUT) ** 0.5
    def coef_of(c):
        return scales[pl.ds(c * LANES, LANES)].reshape(1, LANES) * norm_factor

    def lookup(which, idx):
        low = lax.bitwise_and(idx, LANES - 1)
        first = jnp.take_along_axis(table[which, :, 0:LANES], low, axis=1, mode="promise_in_bounds")
        second = jnp.take_along_axis(table[which, :, LANES:KCODE], low, axis=1, mode="promise_in_bounds")
        return jnp.where(idx >= LANES, second, first)

    unroll = min(UNROLL, groups)

    def decode(c):
        cols = pl.ds(c * LANES, LANES)
        co = coef_of(c)

        @pl.loop(0, groups // unroll)
        def _(q):
            at = pl.ds(pl.multiple_of(q * unroll, unroll), unroll)
            c0 = codes[0, at, cols]
            c1 = codes[1, at, cols]
            out = []
            for g in range(unroll):
                d = lookup(0, jnp.broadcast_to(c0[g : g + 1], (8, LANES))) + lookup(
                    1, jnp.broadcast_to(c1[g : g + 1], (8, LANES))
                )
                out.append(d)
            d = jnp.concatenate(out, axis=0)
            where = pl.ds(pl.multiple_of(q * unroll * 8, unroll * 8), unroll * 8)
            dec[where, cols] = d
            wts[where, cols] = (d * co).astype(bf16)

    for c in range(nc):
        pltpu.make_async_copy(
            gy_hbm.at[:, pl.ds(c * LANES, LANES)], gyf.at[c, rows_of(iz)], loc_sem.at[c]
        ).wait()
    pltpu.make_async_copy(x_hbm, xf.at[jd], loc_sem.at[nc]).wait()
    pl.semaphore_wait(barrier, 2 + nd - 1)

    def send_right(s, c):
        block = lax.rem(iz - s + nz, nz)
        part = gyf.at[c, rows_of(block)]
        return remote(part, part, gy_send.at[0, s], gy_recv.at[0, s, c], din=right)

    def send_left(s, c):
        block = lax.rem(iz + s, nz)
        part = gyf.at[c, rows_of(block)]
        return remote(part, part, gy_send.at[1, s], gy_recv.at[1, s, c], din=left)

    def send_own(c):
        if half > 1 or goes_right[c]:
            send_right(0, c).start()
        if half > 1 or not goes_right[c]:
            send_left(0, c).start()

    for c in range(nc):
        send_own(c)

    def x_copy(k, dev, sem):
        return remote(xf.at[k], xf.at[k], x_send.at[sem], x_recv.at[k], dout=dev)

    x_copy(jd, mate, 2 * chips - 2).start()
    for k in range(1, chips):
        x_copy(jd, 2 * lax.rem(chip + k, chips) + core, k - 1).start()

    def x_forward(k):
        src = 2 * lax.rem(chip + chips - k, chips) + core
        x_copy(src, mate, chips - 1 + k - 1).wait_recv()
        x_copy(src, mate, chips - 1 + k - 1).start()

    def ring(r, c):
        bl = lax.rem(iz - r + nz, nz)
        br = lax.rem(iz + r, nz)
        if r < half or goes_right[c]:
            part = gyf.at[c, rows_of(bl)]
            remote(part, part, gy_send.at[0, 0], gy_recv.at[0, r - 1, c], din=right).wait_recv()
            if r < half - 1 or (r == half - 1 and goes_right[c]):
                send_right(r, c).start()
        if r < half or not goes_right[c]:
            part = gyf.at[c, rows_of(br)]
            remote(part, part, gy_send.at[1, 0], gy_recv.at[1, r - 1, c], din=left).wait_recv()
            if r < half - 1 or (r == half - 1 and not goes_right[c]):
                send_left(r, c).start()

    def g_dot(block, chunks):
        lhs = jnp.concatenate([gyf[c, rows_of(block)] for c in chunks], axis=1)
        rhs = wts[:, pl.ds(chunks[0] * LANES, len(chunks) * LANES)]
        return lax.dot_general(lhs, rhs, (((1,), (1,)), ((), ())), preferred_element_type=f32)

    def g_early(block, slot):
        gkeep[slot] = g_dot(block, early).reshape(2, rows // 2, feats)

    def g_late(block, slot):
        g = gkeep[slot] + g_dot(block, late).reshape(2, rows // 2, feats)
        gkeep[slot] = g
        gst[slot] = g.astype(bf16)
        remote(gst.at[slot, 1 - core], gpr.at[slot], p_send.at[slot], p_recv.at[slot], dout=mate).start()

    def g_pass(block, slot):
        remote(gst.at[slot, 1 - core], gpr.at[slot], p_send.at[slot], p_recv.at[slot], dout=mate).wait_recv()
        total = gkeep[slot, core] + gpr[slot].astype(f32)
        rss[slot] = total.astype(bf16)
        gkeep[slot, core] = total
        by, bx = block // across, lax.rem(block, across)

        @pl.when(bx != my_x)
        def _():
            remote(
                rss.at[slot], rsx.at[by, my_x], r_send.at[slot], r_recv.at[by, my_x],
                dout=2 * (my_y * across + bx) + core,
            ).start()

    def g_sum(block, slot):
        by, bx = block // across, lax.rem(block, across)

        @pl.when(bx == my_x)
        def _():
            acc = gkeep[slot, core]
            for k in range(1, across):
                src = lax.rem(my_x + k, across)
                remote(
                    rss.at[slot], rsx.at[by, src], r_send.at[slot], r_recv.at[by, src], dout=mate
                ).wait_recv()
                acc = acc + rsx[by, src].astype(f32)
            rsy[by] = acc.astype(bf16)

            @pl.when(by != my_y)
            def _():
                remote(rsy.at[by], rsr.at[my_y], y_send.at[by], y_recv.at[my_y], dout=2 * block + core).start()

    def left_of(r):
        return lax.rem(iz - r + nz, nz)

    def right_of(r):
        return lax.rem(iz + r, nz)

    def gw_pair(q, chunks):
        b0, b1 = right_of(q), left_of(q + 1)
        lhs = jnp.concatenate([xt[b0], xt[b1]], axis=1)
        for c in chunks:
            rhs = jnp.concatenate([gyf[c, rows_of(b0)], gyf[c, rows_of(b1)]], axis=0)
            d = jnp.dot(lhs, rhs, preferred_element_type=f32)
            cols = pl.ds(c * LANES, LANES)
            if q == 0:
                gw[:, cols] = d
            else:
                gw[:, cols] += d

    def transpose_x(k):
        blk = xf[pl.ds(2 * k, 2)].reshape(rows, feats)
        xt[k] = jnp.transpose(blk)

    def x_ready(k):
        src = 2 * k + 1 - core
        x_copy(src, mate, 0).wait_recv()
        transpose_x(k)

    hloc[...] = jnp.zeros_like(hloc)
    sown[...] = jnp.zeros_like(sown)
    rows16 = lax.broadcasted_iota(jnp.int32, (16, LANES), 0)
    row_low = [(rows16 // 8 + 2 * n).astype(f32).astype(bf16) for n in range(LOW // 2)]
    row_high = [(rows16 + 16 * n).astype(f32).astype(bf16) for n in range(HIGH // 16)]
    zero16 = jnp.zeros((16, LANES), bf16)
    one16 = jnp.ones((16, LANES), bf16)

    def scale_part(c):
        cols = pl.ds(c * LANES, LANES)
        sown[c : c + 1, :] = jnp.sum(dec[:, cols] * gw[:, cols], axis=0, keepdims=True)

    def piece(c, q):
        cols = pl.ds(c * LANES, LANES)
        co = coef_of(c)
        if True:
            at = pl.ds(pl.multiple_of(q * unroll, unroll), unroll)
            s = gw[pl.ds(pl.multiple_of(q * unroll * 8, unroll * 8), unroll * 8), cols] * co
            for b in range(BOOKS):
                cd = codes[b, at, cols]
                lo = lax.shift_right_logical(cd, HBITS).astype(f32)
                hi = lax.bitwise_and(cd, HIGH - 1).astype(f32)
                a, o = [], []
                for g in range(unroll):
                    sg = s[8 * g : 8 * g + 8]
                    two = jnp.concatenate([sg, sg], axis=0).astype(bf16)
                    lo_b = jnp.broadcast_to(lo[g : g + 1], (16, LANES)).astype(bf16)
                    a.append(jnp.concatenate([jnp.where(lo_b == r, two, zero16) for r in row_low], axis=0))
                    hi_b = jnp.broadcast_to(hi[g : g + 1], (16, LANES)).astype(bf16)
                    o.append(jnp.concatenate([jnp.where(hi_b == r, one16, zero16) for r in row_high], axis=0))
                left_m = jnp.concatenate(a, axis=1)
                right_m = jnp.concatenate(o, axis=1)
                hloc[b] += lax.dot_general(
                    right_m, left_m, (((1,), (1,)), ((), ())), preferred_element_type=f32
                )

    def finish(c):
        scale_part(c)

        @pl.loop(0, groups // unroll)
        def _(q):
            piece(c, q)

    for n, (src, dst) in enumerate(operands):
        pltpu.make_async_copy(src, dst, loc_sem.at[nc + 1 + n]).wait()
    for b in range(BOOKS):
        table[b] = books[b].astype(bf16).astype(f32)
    todo = []

    def add(at, job, *args):
        todo.append((at, functools.partial(job, *args)))

    def sides(r):
        pairs = []
        if r == 0:
            pairs.append((lambda: iz, 0))
        else:
            pairs.append((lambda: left_of(r), 2 * r - 1))
            if r < half:
                pairs.append((lambda: right_of(r), 2 * r))
        return pairs

    def on_sides(job, r):
        for block, slot in sides(r):
            job(block(), slot)

    def one_side(job, r, n):
        block, slot = sides(r)[n]
        job(block(), slot)

    for c in range(nc):
        add((0, 0, 1, 1, 1, 2, 2)[c], decode, c)
    for k in range(1, chips):
        add(4, x_forward, k)
    for k in range(chips):
        add(5, x_ready, k)
    when_early = (3, 3, 3, 4, 5, 6, 7, 8, 9)
    when_late = (4, 4, 5, 6, 7, 8, 9, 10, 11)
    for r in range(half + 1):
        for n in range(len(sides(r))):
            add(when_early[r], one_side, g_early, r, n)
    for r in range(half - 1):
        add(when_late[r] + 1, on_sides, g_pass, r)
        if r < half - 2:
            add(when_late[r] + 2, on_sides, g_sum, r)
    for r in range(half + 1):
        for n in range(len(sides(r))):
            add(when_late[r], one_side, g_late, r, n)
    for q in range(half):
        add((6, 6, 6, 7, 7, 7, 8, 9)[q], gw_pair, q, early)
    for q in range(half):
        add((6, 6, 7, 7, 8, 9, 10, 11)[q], gw_pair, q, late)
    shown = [(c, q) for c in early for q in range(groups // unroll)]
    hidden = shown[:11]
    for n, (c, q) in enumerate(hidden):
        if q == 0:
            add(9 if n < 5 else 10, scale_part, c)
        add(9 if n < 5 else 10, piece, c, q)
    for at, job in todo:
        if at == 0:
            job()
    last = half + skew
    for v in range(1, last + 1):
        ops = []
        if v <= half:
            ops += [functools.partial(ring, v, c) for c in early]
        if 1 <= v - skew <= half:
            ops += [functools.partial(ring, v - skew, c) for c in late]
        jobs = [job for at, job in todo if at == v]
        slots = len(ops)
        for n, op in enumerate(ops):
            op()
            for job in jobs[n * len(jobs) // slots : (n + 1) * len(jobs) // slots]:
                job()
    for at, job in todo:
        if at == last + 1:
            job()
    on_sides(g_pass, half - 1)
    on_sides(g_sum, half - 2)
    for c, q in shown[11:12]:
        piece(c, q)
    for n, c in enumerate(early[3:] + late):
        finish(c)
        if n == 0:
            on_sides(g_pass, half)
        if n == 2:
            on_sides(g_sum, half - 1)

    def s_copy(k):
        dev = lax.rem(iz + k, nz)
        return remote(sown, sz.at[iz], s_send.at[k - 1], s_recv.at[iz], din=dev)

    for k in range(1, nz):
        s_copy(k).start()

    pieces = hfin.shape[0]
    mine = lax.rem(jd, pieces)
    for b in range(BOOKS):
        turned = jnp.transpose(hloc[b])
        for h in range(2):
            part = jnp.concatenate(
                [turned[8 * n : 8 * n + 8, :] for n in range(LOW // 2 * h, LOW // 2 * (h + 1))], axis=1
            )
            hbk[4 * b + 2 * h] = part[0:4]
            hbk[4 * b + 2 * h + 1] = part[4:8]

    def h_copy(k):
        other = lax.rem(jd + k, nd)
        return remote(
            hbk.at[lax.rem(other, pieces)], hplane.at[jd], hx_send.at[k - 1], hx_recv.at[jd], dout=other
        )

    for k in range(1, nd):
        h_copy(k).start()
    hplane[jd] = hbk[mine]
    on_sides(g_sum, half)
    for k in range(1, nd):
        src = lax.rem(jd + nd - k, nd)
        remote(hbk.at[0], hplane.at[src], hx_send.at[0], hx_recv.at[src], dout=src).wait_recv()
    hz[iz] = jnp.sum(hplane[...], axis=0)

    def z_copy(k):
        dev = lax.rem(iz + k, nz)
        return remote(hz.at[iz], hz.at[iz], hz_send.at[k - 1], hz_recv.at[iz], din=dev)

    for k in range(1, nz):
        z_copy(k).start()

    sz[iz] = sown[...]
    for k in range(1, nz):
        src = lax.rem(iz + nz - k, nz)
        remote(sown, sz.at[src], s_send.at[0], s_recv.at[src], din=src).wait_recv()
    scale_out[...] = jnp.sum(sz[...], axis=0)

    acc = rsy[my_y].astype(f32)
    for k in range(1, chips // across):
        src = lax.rem(my_y + k, chips // across)
        remote(rsy.at[0], rsr.at[src], y_send.at[0], y_recv.at[src], dout=mate).wait_recv()
        acc = acc + rsr[src].astype(f32)
    gx_out[...] = acc.astype(bf16)

    for k in range(1, nz):
        src = lax.rem(iz + nz - k, nz)
        remote(hz.at[src], hz.at[src], hz_send.at[0], hz_recv.at[src], din=src).wait_recv()
    hfin[mine] = jnp.sum(hz[...], axis=0)

    def f_copy(k):
        dev = jd - mine + lax.rem(mine + k, pieces)
        return remote(hfin.at[mine], hfin.at[mine], hf_send.at[k - 1], hf_recv.at[mine], dout=dev)

    for k in range(1, pieces):
        f_copy(k).start()
    for k in range(1, pieces):
        src = lax.rem(mine + k, pieces)
        remote(hfin.at[src], hfin.at[src], hf_send.at[0], hf_recv.at[src], dout=mate).wait_recv()
    for b in range(BOOKS):
        for h in range(2):
            book_out[b, :, pl.ds(h * LANES, LANES)] = jnp.concatenate(
                [hfin[4 * b + 2 * h], hfin[4 * b + 2 * h + 1]], axis=0
            )

    for s in range(half):
        wr = gyf.at[pl.ds(0, nc if s < half - 1 else n_right), rows_of(left_of(s))]
        remote(wr, wr, gy_send.at[0, s], gy_recv.at[0, s, 0], din=right).wait_send()
        if s < half - 1:
            wl = gyf.at[:, rows_of(right_of(s))]
        else:
            wl = gyf.at[pl.ds(0, nc - n_right), rows_of(right_of(s))]
        if s < half - 1 or nc > n_right:
            remote(wl, wl, gy_send.at[1, s], gy_recv.at[1, s, 0], din=left).wait_send()
    for k in range(2 * chips - 1):
        x_copy(jd, mate, k).wait_send()
    for k in range(1, nz):
        s_copy(k).wait_send()
        z_copy(k).wait_send()
    for k in range(1, nd):
        h_copy(k).wait_send()
    for k in range(1, pieces):
        f_copy(k).wait_send()
    for k in range(nz):
        remote(gst.at[k, 1 - core], gpr.at[k], p_send.at[k], p_recv.at[k], dout=mate).wait_send()

        block = iz if k == 0 else (left_of((k + 1) // 2) if k % 2 else right_of(k // 2))

        @pl.when(lax.rem(block, across) != my_x)
        def _():
            remote(rss.at[k], rsx.at[0, 0], r_send.at[k], r_recv.at[0, 0], dout=mate).wait_send()

    for k in range(chips // across):
        @pl.when(k != my_y)
        def _():
            remote(rsy.at[k], rsr.at[0], y_send.at[k], y_recv.at[0], dout=mate).wait_send()


def fused(nz, nd, x, gy, codes, books, scales):
    xrows, feats = x.shape
    rows, outs = gy.shape
    nc = outs // LANES
    chips = nd // 2
    half = nz // 2
    bf16, f32 = jnp.bfloat16, jnp.float32
    V = pltpu.VMEM
    D = pltpu.SemaphoreType.DMA
    vm = pl.BlockSpec(memory_space=pltpu.VMEM)
    anyspec = pl.BlockSpec(memory_space=pl.ANY)
    tile = (GROUP // 2, LANES)
    scratch = [
        V(codes.shape, jnp.int32),
        V(books.shape, f32),
        V(scales.shape, f32),
        V((nc, rows * nz, LANES), bf16),
        V((nd, xrows, feats), bf16),
        V((nz, feats, rows), bf16),
        V((feats, outs), bf16),
        V((feats, outs), f32),
        V((feats, outs), f32),
        V((BOOKS, GROUP, KCODE), f32),
        V((nz, 2, rows // 2, feats), f32),
        V((nz, 2, rows // 2, feats), bf16),
        V((nz, rows // 2, feats), bf16),
        V((nz, rows // 2, feats), bf16),
        V((chips // 4, 4, rows // 2, feats), bf16),
        V((chips // 4, rows // 2, feats), bf16),
        V((chips // 4, rows // 2, feats), bf16),
        V((BOOKS, HIGH, LOW * 8), f32),
        V((8,) + tile, f32),
        V((nd,) + tile, f32),
        V((nz,) + tile, f32),
        V((8,) + tile, f32),
        V((8, LANES), f32),
        V((nz, 8, LANES), f32),
        D((nc + 4,)),
        D((2, half)),
        D((2, half, nc)),
        D((2 * chips - 1,)),
        D((nd,)),
        D((nz,)),
        D((nz,)),
        D((nz,)),
        D((chips // 4, 4)),
        D((chips // 4,)),
        D((chips // 4,)),
        D((nd,)),
        D((nd,)),
        D((nz,)),
        D((nz,)),
        D((8,)),
        D((8,)),
        D((nz,)),
        D((nz,)),
    ]
    return pl.pallas_call(
        functools.partial(kernel, nz, nd),
        out_shape=(
            jax.ShapeDtypeStruct((xrows, feats), bf16),
            jax.ShapeDtypeStruct((BOOKS, GROUP, KCODE), f32),
            jax.ShapeDtypeStruct((8, LANES), f32),
        ),
        in_specs=[anyspec] * 5,
        out_specs=(vm, vm, vm),
        scratch_shapes=scratch,
        compiler_params=pltpu.CompilerParams(
            collective_id=0, has_side_effects=True, vmem_limit_bytes=60 * 1024 * 1024
        ),
        name="fused",
    )(x, gy, codes, books, scales)


def local(nz, nd, inputs, cotangent, codes, codebooks, scales, book_mean, book_var, scale_mean, scale_var):
    norm_factor = 1.0 / (2.0 * DOUT) ** 0.5
    loss_scale = (TOKENS * DIN / 4096.0) ** 0.5
    outs = scales.shape[0]
    gx, book, scale = fused(nz, nd, inputs, cotangent, codes, jnp.transpose(codebooks, (0, 2, 1)), scales)
    book_grad = jnp.transpose(book, (0, 2, 1)) / loss_scale
    scale_grad = scale[: outs // LANES].reshape(outs) * norm_factor / loss_scale
    new_books, new_book_mean, new_book_var = adam_step(codebooks, book_mean, book_var, book_grad)
    new_scales, new_scale_mean, new_scale_var = adam_step(scales, scale_mean, scale_var, scale_grad)
    return (
        gx,
        book_grad,
        new_books,
        new_book_mean,
        new_book_var,
        new_scales,
        new_scale_mean,
        new_scale_var,
    )


def solution(mesh):
    nz, nd = mesh.shape["din"], mesh.shape["dout"]
    in_specs = (
        P("dout", "din"),
        P("din", "dout"),
        P(None, "din", "dout"),
        P(),
        P("dout"),
        P(),
        P(),
        P("dout"),
        P("dout"),
    )
    out_specs = (P("dout", "din"), P(), P(), P(), P(), P("dout"), P("dout"), P("dout"))
    return jax.shard_map(
        functools.partial(local, nz, nd), mesh=mesh, in_specs=in_specs, out_specs=out_specs, check_vma=False
    )
```

```python
import functools

import jax
import jax.numpy as jnp
from jax import lax
from jax.experimental import pallas as pl
from jax.experimental.pallas import tpu as pltpu
from jax.sharding import PartitionSpec as P

DIN = 8192
DOUT = 28672
KCODE = 256
BOOKS = 2
GROUP = 8
TOKENS = 2048

beta_one = 0.9
beta_two = 0.999
adam_rate = 0.01
adam_eps = 1e-08
corr_one = 1.0 - 0.9**10
corr_two = 1.0 - 0.999**10

LANES = 128
LOW = 8
HBITS = 5
SKEW = 1
UNROLL = 16
HIGH = KCODE // LOW


def adam_step(param, mean_old, var_old, gradient):
    mean_new = beta_one * mean_old + (1.0 - beta_one) * gradient
    var_new = beta_two * var_old + (1.0 - beta_two) * gradient * gradient
    update = mean_new / corr_one / (jnp.sqrt(var_new / corr_two) + adam_eps)
    return (param - adam_rate * update, mean_new, var_new)


def kernel(
    nz, nd, x_hbm, gy_hbm, codes_hbm, books_hbm, scales_hbm, gx_out, book_out, scale_out,
    codes, books, scales, gyf, xf, xt, wts, dec, gw, table, gkeep, gst, gpr, rss, rsr, hloc, hbk, hplane, hz, hfin, sown, sz,
    loc_sem, gy_send, gy_recv, x_send, x_recv, p_send, p_recv, r_send, r_recv,
    hx_send, hx_recv, hz_send, hz_recv, hf_send, hf_recv, s_send, s_recv,
):
    chips = nd // 2
    half = nz // 2
    nc = gyf.shape[0]
    early = list(range((nc + 1) // 2))
    late = list(range((nc + 1) // 2, nc))
    goes_right = [k % 2 == 0 for k in range(nc)]
    n_right = sum(goes_right)
    skew = min(SKEW, half - 1)
    rows = gy_hbm.shape[0]
    xrows = x_hbm.shape[0]
    feats = x_hbm.shape[1]
    groups = codes.shape[1]
    iz = lax.axis_index("din")
    jd = lax.axis_index("dout")
    chip = jd // 2
    core = jd % 2
    mate = jd + 1 - 2 * core
    right = lax.rem(iz + 1, nz)
    left = lax.rem(iz + nz - 1, nz)
    f32 = jnp.float32
    bf16 = jnp.bfloat16

    def remote(src, dst, ssem, rsem, din=None, dout=None):
        where = {}
        if din is not None:
            where["din"] = din
        if dout is not None:
            where["dout"] = dout
        return pltpu.make_async_remote_copy(
            src_ref=src, dst_ref=dst, send_sem=ssem, recv_sem=rsem,
            device_id=where, device_id_type=pl.DeviceIdType.MESH,
        )

    def rows_of(block):
        return pl.ds(pl.multiple_of(block * rows, rows), rows)

    barrier = pltpu.get_barrier_semaphore()
    for dev in (right, left):
        pl.semaphore_signal(barrier, 1, device_id={"din": dev}, device_id_type=pl.DeviceIdType.MESH)
    for k in range(1, nd):
        pl.semaphore_signal(barrier, 1, device_id={"dout": lax.rem(jd + k, nd)}, device_id_type=pl.DeviceIdType.MESH)

    for c in range(nc):
        pltpu.make_async_copy(
            gy_hbm.at[:, pl.ds(c * LANES, LANES)], gyf.at[c, rows_of(iz)], loc_sem.at[c]
        ).start()
    pltpu.make_async_copy(x_hbm, xf.at[jd], loc_sem.at[nc]).start()
    operands = ((codes_hbm, codes), (books_hbm, books), (scales_hbm, scales))
    for n, (src, dst) in enumerate(operands):
        pltpu.make_async_copy(src, dst, loc_sem.at[nc + 1 + n]).start()

    norm_factor = 1.0 / (2.0 * DOUT) ** 0.5
    def coef_of(c):
        return scales[pl.ds(c * LANES, LANES)].reshape(1, LANES) * norm_factor

    def lookup(which, idx):
        low = lax.bitwise_and(idx, LANES - 1)
        first = jnp.take_along_axis(table[which, :, 0:LANES], low, axis=1, mode="promise_in_bounds")
        second = jnp.take_along_axis(table[which, :, LANES:KCODE], low, axis=1, mode="promise_in_bounds")
        return jnp.where(idx >= LANES, second, first)

    unroll = min(UNROLL, groups)

    def decode(c):
        cols = pl.ds(c * LANES, LANES)
        co = coef_of(c)

        @pl.loop(0, groups // unroll)
        def _(q):
            at = pl.ds(pl.multiple_of(q * unroll, unroll), unroll)
            c0 = codes[0, at, cols]
            c1 = codes[1, at, cols]
            out = []
            for g in range(unroll):
                d = lookup(0, jnp.broadcast_to(c0[g : g + 1], (8, LANES))) + lookup(
                    1, jnp.broadcast_to(c1[g : g + 1], (8, LANES))
                )
                out.append(d)
            d = jnp.concatenate(out, axis=0)
            where = pl.ds(pl.multiple_of(q * unroll * 8, unroll * 8), unroll * 8)
            dec[where, cols] = d
            wts[where, cols] = (d * co).astype(bf16)

    for c in range(nc):
        pltpu.make_async_copy(
            gy_hbm.at[:, pl.ds(c * LANES, LANES)], gyf.at[c, rows_of(iz)], loc_sem.at[c]
        ).wait()
    pltpu.make_async_copy(x_hbm, xf.at[jd], loc_sem.at[nc]).wait()
    pl.semaphore_wait(barrier, 2 + nd - 1)

    def send_right(s, c):
        block = lax.rem(iz - s + nz, nz)
        part = gyf.at[c, rows_of(block)]
        return remote(part, part, gy_send.at[0, s], gy_recv.at[0, s, c], din=right)

    def send_left(s, c):
        block = lax.rem(iz + s, nz)
        part = gyf.at[c, rows_of(block)]
        return remote(part, part, gy_send.at[1, s], gy_recv.at[1, s, c], din=left)

    def send_own(c):
        if half > 1 or goes_right[c]:
            send_right(0, c).start()
        if half > 1 or not goes_right[c]:
            send_left(0, c).start()

    for c in range(nc):
        send_own(c)

    def x_copy(k, dev, sem):
        return remote(xf.at[k], xf.at[k], x_send.at[sem], x_recv.at[k], dout=dev)

    x_copy(jd, mate, 2 * chips - 2).start()
    for k in range(1, chips):
        x_copy(jd, 2 * lax.rem(chip + k, chips) + core, k - 1).start()

    def x_forward(k):
        src = 2 * lax.rem(chip + chips - k, chips) + core
        x_copy(src, mate, chips - 1 + k - 1).wait_recv()
        x_copy(src, mate, chips - 1 + k - 1).start()

    def ring(r, c):
        bl = lax.rem(iz - r + nz, nz)
        br = lax.rem(iz + r, nz)
        if r < half or goes_right[c]:
            part = gyf.at[c, rows_of(bl)]
            remote(part, part, gy_send.at[0, 0], gy_recv.at[0, r - 1, c], din=right).wait_recv()
            if r < half - 1 or (r == half - 1 and goes_right[c]):
                send_right(r, c).start()
        if r < half or not goes_right[c]:
            part = gyf.at[c, rows_of(br)]
            remote(part, part, gy_send.at[1, 0], gy_recv.at[1, r - 1, c], din=left).wait_recv()
            if r < half - 1 or (r == half - 1 and not goes_right[c]):
                send_left(r, c).start()

    def g_dot(block, chunks):
        lhs = jnp.concatenate([gyf[c, rows_of(block)] for c in chunks], axis=1)
        rhs = wts[:, pl.ds(chunks[0] * LANES, len(chunks) * LANES)]
        return lax.dot_general(lhs, rhs, (((1,), (1,)), ((), ())), preferred_element_type=f32)

    def g_early(block, slot):
        gkeep[slot] = g_dot(block, early).reshape(2, rows // 2, feats)

    def g_late(block, slot):
        g = gkeep[slot] + g_dot(block, late).reshape(2, rows // 2, feats)
        gkeep[slot] = g
        gst[slot] = g.astype(bf16)
        remote(gst.at[slot, 1 - core], gpr.at[slot], p_send.at[slot], p_recv.at[slot], dout=mate).start()

    def g_pass(block, slot):
        remote(gst.at[slot, 1 - core], gpr.at[slot], p_send.at[slot], p_recv.at[slot], dout=mate).wait_recv()
        total = gkeep[slot, core] + gpr[slot].astype(f32)
        rss[slot] = total.astype(bf16)

        @pl.when(block == chip)
        def _():
            pltpu.make_async_copy(rss.at[slot], rsr.at[chip], r_send.at[slot]).start()

        @pl.when(block != chip)
        def _():
            remote(rss.at[slot], rsr.at[chip], r_send.at[slot], r_recv.at[chip], dout=2 * block + core).start()

    def left_of(r):
        return lax.rem(iz - r + nz, nz)

    def right_of(r):
        return lax.rem(iz + r, nz)

    def gw_pair(q, chunks):
        b0, b1 = right_of(q), left_of(q + 1)
        lhs = jnp.concatenate([xt[b0], xt[b1]], axis=1)
        for c in chunks:
            rhs = jnp.concatenate([gyf[c, rows_of(b0)], gyf[c, rows_of(b1)]], axis=0)
            d = jnp.dot(lhs, rhs, preferred_element_type=f32)
            cols = pl.ds(c * LANES, LANES)
            if q == 0:
                gw[:, cols] = d
            else:
                gw[:, cols] += d

    def transpose_x(k):
        blk = xf[pl.ds(2 * k, 2)].reshape(rows, feats)
        xt[k] = jnp.transpose(blk)

    def x_ready(k):
        src = 2 * k + 1 - core
        x_copy(src, mate, 0).wait_recv()
        transpose_x(k)

    hloc[...] = jnp.zeros_like(hloc)
    sown[...] = jnp.zeros_like(sown)
    rows16 = lax.broadcasted_iota(jnp.int32, (16, LANES), 0)
    row_low = [(rows16 // 8 + 2 * n).astype(f32).astype(bf16) for n in range(LOW // 2)]
    row_high = [(rows16 + 16 * n).astype(f32).astype(bf16) for n in range(HIGH // 16)]
    zero16 = jnp.zeros((16, LANES), bf16)
    one16 = jnp.ones((16, LANES), bf16)

    def scale_part(c):
        cols = pl.ds(c * LANES, LANES)
        sown[c : c + 1, :] = jnp.sum(dec[:, cols] * gw[:, cols], axis=0, keepdims=True)

    def piece(c, q):
        cols = pl.ds(c * LANES, LANES)
        co = coef_of(c)
        if True:
            at = pl.ds(pl.multiple_of(q * unroll, unroll), unroll)
            s = gw[pl.ds(pl.multiple_of(q * unroll * 8, unroll * 8), unroll * 8), cols] * co
            for b in range(BOOKS):
                cd = codes[b, at, cols]
                lo = lax.shift_right_logical(cd, HBITS).astype(f32)
                hi = lax.bitwise_and(cd, HIGH - 1).astype(f32)
                a, o = [], []
                for g in range(unroll):
                    sg = s[8 * g : 8 * g + 8]
                    two = jnp.concatenate([sg, sg], axis=0).astype(bf16)
                    lo_b = jnp.broadcast_to(lo[g : g + 1], (16, LANES)).astype(bf16)
                    a.append(jnp.concatenate([jnp.where(lo_b == r, two, zero16) for r in row_low], axis=0))
                    hi_b = jnp.broadcast_to(hi[g : g + 1], (16, LANES)).astype(bf16)
                    o.append(jnp.concatenate([jnp.where(hi_b == r, one16, zero16) for r in row_high], axis=0))
                left_m = jnp.concatenate(a, axis=1)
                right_m = jnp.concatenate(o, axis=1)
                hloc[b] += lax.dot_general(
                    right_m, left_m, (((1,), (1,)), ((), ())), preferred_element_type=f32
                )

    def finish(c):
        scale_part(c)

        @pl.loop(0, groups // unroll)
        def _(q):
            piece(c, q)

    for n, (src, dst) in enumerate(operands):
        pltpu.make_async_copy(src, dst, loc_sem.at[nc + 1 + n]).wait()
    for b in range(BOOKS):
        table[b] = books[b].astype(bf16).astype(f32)
    todo = []

    def add(at, job, *args):
        todo.append((at, functools.partial(job, *args)))

    def sides(r):
        pairs = []
        if r == 0:
            pairs.append((lambda: iz, 0))
        else:
            pairs.append((lambda: left_of(r), 2 * r - 1))
            if r < half:
                pairs.append((lambda: right_of(r), 2 * r))
        return pairs

    def on_sides(job, r):
        for block, slot in sides(r):
            job(block(), slot)

    def one_side(job, r, n):
        block, slot = sides(r)[n]
        job(block(), slot)

    for c in range(nc):
        add((0, 0, 1, 1, 1, 2, 2)[c], decode, c)
    for k in range(1, chips):
        add(3, x_forward, k)
    for k in range(chips):
        add(4, x_ready, k)
    when_early = (2, 3, 3, 4, 5, 6, 7, 8, 9)
    when_late = (3, 3, 4, 5, 6, 7, 8, 9, 10)
    for r in range(half + 1):
        for n in range(len(sides(r))):
            add(when_early[r], one_side, g_early, r, n)
    for r in range(half - 1):
        add(when_late[r] + 1, on_sides, g_pass, r)
    for r in range(half + 1):
        for n in range(len(sides(r))):
            add(when_late[r], one_side, g_late, r, n)
    for q in range(half):
        add((5, 5, 5, 6, 6, 7, 8, 9)[q], gw_pair, q, early)
    for q in range(half):
        add((5, 5, 6, 6, 7, 8, 9, 10)[q], gw_pair, q, late)
    hidden = min(3, groups // unroll)
    add(9, scale_part, early[0])
    for q in range(hidden):
        add(9, piece, early[0], q)
    for at, job in todo:
        if at == 0:
            job()
    last = half + skew
    for v in range(1, last + 1):
        ops = []
        if v <= half:
            ops += [functools.partial(ring, v, c) for c in early]
        if 1 <= v - skew <= half:
            ops += [functools.partial(ring, v - skew, c) for c in late]
        jobs = [job for at, job in todo if at == v]
        slots = len(ops)
        for n, op in enumerate(ops):
            op()
            for job in jobs[n * len(jobs) // slots : (n + 1) * len(jobs) // slots]:
                job()
    for at, job in todo:
        if at == last + 1:
            job()
    for n, c in enumerate(early + late):
        if n == 0:
            for q in range(hidden, groups // unroll):
                piece(c, q)
        else:
            finish(c)
        if n == 1:
            on_sides(g_pass, half - 1)
        if n == 2:
            g_pass(left_of(half), 2 * half - 1)

    def s_copy(k):
        dev = lax.rem(iz + k, nz)
        return remote(sown, sz.at[iz], s_send.at[k - 1], s_recv.at[iz], din=dev)

    for k in range(1, nz):
        s_copy(k).start()

    pieces = hfin.shape[0]
    mine = lax.rem(jd, pieces)
    for b in range(BOOKS):
        turned = jnp.transpose(hloc[b])
        for h in range(2):
            part = jnp.concatenate(
                [turned[8 * n : 8 * n + 8, :] for n in range(LOW // 2 * h, LOW // 2 * (h + 1))], axis=1
            )
            hbk[4 * b + 2 * h] = part[0:4]
            hbk[4 * b + 2 * h + 1] = part[4:8]

    def h_copy(k):
        other = lax.rem(jd + k, nd)
        return remote(
            hbk.at[lax.rem(other, pieces)], hplane.at[jd], hx_send.at[k - 1], hx_recv.at[jd], dout=other
        )

    for k in range(1, nd):
        h_copy(k).start()
    hplane[jd] = hbk[mine]
    for k in range(1, nd):
        src = lax.rem(jd + nd - k, nd)
        remote(hbk.at[0], hplane.at[src], hx_send.at[0], hx_recv.at[src], dout=src).wait_recv()
    hz[iz] = jnp.sum(hplane[...], axis=0)

    def z_copy(k):
        dev = lax.rem(iz + k, nz)
        return remote(hz.at[iz], hz.at[iz], hz_send.at[k - 1], hz_recv.at[iz], din=dev)

    for k in range(1, nz):
        z_copy(k).start()

    sz[iz] = sown[...]
    for k in range(1, nz):
        src = lax.rem(iz + nz - k, nz)
        remote(sown, sz.at[src], s_send.at[0], s_recv.at[src], din=src).wait_recv()
    scale_out[...] = jnp.sum(sz[...], axis=0)

    for k in range(1, chips):
        src = lax.rem(chip + chips - k, chips)
        remote(rss.at[0], rsr.at[src], r_send.at[0], r_recv.at[src], dout=2 * src + core).wait_recv()
    slot_own = 0
    dist = lax.rem(chip - iz + nz, nz)
    slot_own = jnp.where(dist == 0, 0, jnp.where(dist < half, 2 * dist, 2 * (nz - dist) - 1))
    pltpu.make_async_copy(rss.at[slot_own], rsr.at[chip], r_send.at[slot_own]).wait()
    acc = rsr[0].astype(f32)
    for k in range(1, chips):
        acc = acc + rsr[k].astype(f32)
    gx_out[...] = acc.astype(bf16)

    for k in range(1, nz):
        src = lax.rem(iz + nz - k, nz)
        remote(hz.at[src], hz.at[src], hz_send.at[0], hz_recv.at[src], din=src).wait_recv()
    hfin[mine] = jnp.sum(hz[...], axis=0)

    def f_copy(k):
        dev = jd - mine + lax.rem(mine + k, pieces)
        return remote(hfin.at[mine], hfin.at[mine], hf_send.at[k - 1], hf_recv.at[mine], dout=dev)

    for k in range(1, pieces):
        f_copy(k).start()
    for k in range(1, pieces):
        src = lax.rem(mine + k, pieces)
        remote(hfin.at[src], hfin.at[src], hf_send.at[0], hf_recv.at[src], dout=mate).wait_recv()
    for b in range(BOOKS):
        for h in range(2):
            book_out[b, :, pl.ds(h * LANES, LANES)] = jnp.concatenate(
                [hfin[4 * b + 2 * h], hfin[4 * b + 2 * h + 1]], axis=0
            )

    for s in range(half):
        wr = gyf.at[pl.ds(0, nc if s < half - 1 else n_right), rows_of(left_of(s))]
        remote(wr, wr, gy_send.at[0, s], gy_recv.at[0, s, 0], din=right).wait_send()
        if s < half - 1:
            wl = gyf.at[:, rows_of(right_of(s))]
        else:
            wl = gyf.at[pl.ds(0, nc - n_right), rows_of(right_of(s))]
        if s < half - 1 or nc > n_right:
            remote(wl, wl, gy_send.at[1, s], gy_recv.at[1, s, 0], din=left).wait_send()
    for k in range(2 * chips - 1):
        x_copy(jd, mate, k).wait_send()
    for k in range(1, nz):
        s_copy(k).wait_send()
        z_copy(k).wait_send()
    for k in range(1, nd):
        h_copy(k).wait_send()
    for k in range(1, pieces):
        f_copy(k).wait_send()
    for k in range(nz):
        remote(gst.at[k, 1 - core], gpr.at[k], p_send.at[k], p_recv.at[k], dout=mate).wait_send()

        @pl.when(k != slot_own)
        def _():
            remote(rss.at[k], rsr.at[chip], r_send.at[k], r_recv.at[chip], dout=mate).wait_send()


def fused(nz, nd, x, gy, codes, books, scales):
    xrows, feats = x.shape
    rows, outs = gy.shape
    nc = outs // LANES
    chips = nd // 2
    half = nz // 2
    bf16, f32 = jnp.bfloat16, jnp.float32
    V = pltpu.VMEM
    D = pltpu.SemaphoreType.DMA
    vm = pl.BlockSpec(memory_space=pltpu.VMEM)
    anyspec = pl.BlockSpec(memory_space=pl.ANY)
    tile = (GROUP // 2, LANES)
    scratch = [
        V(codes.shape, jnp.int32),
        V(books.shape, f32),
        V(scales.shape, f32),
        V((nc, rows * nz, LANES), bf16),
        V((nd, xrows, feats), bf16),
        V((nz, feats, rows), bf16),
        V((feats, outs), bf16),
        V((feats, outs), f32),
        V((feats, outs), f32),
        V((BOOKS, GROUP, KCODE), f32),
        V((nz, 2, rows // 2, feats), f32),
        V((nz, 2, rows // 2, feats), bf16),
        V((nz, rows // 2, feats), bf16),
        V((nz, rows // 2, feats), bf16),
        V((chips, rows // 2, feats), bf16),
        V((BOOKS, HIGH, LOW * 8), f32),
        V((8,) + tile, f32),
        V((nd,) + tile, f32),
        V((nz,) + tile, f32),
        V((8,) + tile, f32),
        V((8, LANES), f32),
        V((nz, 8, LANES), f32),
        D((nc + 4,)),
        D((2, half)),
        D((2, half, nc)),
        D((2 * chips - 1,)),
        D((nd,)),
        D((nz,)),
        D((nz,)),
        D((nz,)),
        D((chips,)),
        D((nd,)),
        D((nd,)),
        D((nz,)),
        D((nz,)),
        D((8,)),
        D((8,)),
        D((nz,)),
        D((nz,)),
    ]
    return pl.pallas_call(
        functools.partial(kernel, nz, nd),
        out_shape=(
            jax.ShapeDtypeStruct((xrows, feats), bf16),
            jax.ShapeDtypeStruct((BOOKS, GROUP, KCODE), f32),
            jax.ShapeDtypeStruct((8, LANES), f32),
        ),
        in_specs=[anyspec] * 5,
        out_specs=(vm, vm, vm),
        scratch_shapes=scratch,
        compiler_params=pltpu.CompilerParams(
            collective_id=0, has_side_effects=True, vmem_limit_bytes=60 * 1024 * 1024
        ),
        name="fused",
    )(x, gy, codes, books, scales)


def local(nz, nd, inputs, cotangent, codes, codebooks, scales, book_mean, book_var, scale_mean, scale_var):
    norm_factor = 1.0 / (2.0 * DOUT) ** 0.5
    loss_scale = (TOKENS * DIN / 4096.0) ** 0.5
    outs = scales.shape[0]
    gx, book, scale = fused(nz, nd, inputs, cotangent, codes, jnp.transpose(codebooks, (0, 2, 1)), scales)
    book_grad = jnp.transpose(book, (0, 2, 1)) / loss_scale
    scale_grad = scale[: outs // LANES].reshape(outs) * norm_factor / loss_scale
    new_books, new_book_mean, new_book_var = adam_step(codebooks, book_mean, book_var, book_grad)
    new_scales, new_scale_mean, new_scale_var = adam_step(scales, scale_mean, scale_var, scale_grad)
    return (
        gx,
        book_grad,
        new_books,
        new_book_mean,
        new_book_var,
        new_scales,
        new_scale_mean,
        new_scale_var,
    )


def solution(mesh):
    nz, nd = mesh.shape["din"], mesh.shape["dout"]
    in_specs = (
        P("dout", "din"),
        P("din", "dout"),
        P(None, "din", "dout"),
        P(),
        P("dout"),
        P(),
        P(),
        P("dout"),
        P("dout"),
    )
    out_specs = (P("dout", "din"), P(), P(), P(), P(), P("dout"), P("dout"), P("dout"))
    return jax.shard_map(
        functools.partial(local, nz, nd), mesh=mesh, in_specs=in_specs, out_specs=out_specs, check_vma=False
    )
```
